32 devices in a mesh: dp: 8 (over z, core), fsdp: 4 (over y, x).
Axes of the slice: x: 2, y: 2, z: 4, core: 2. Of those that a mesh axis runs over, the one named last changes fastest.
Arguments:
- tokens: bfloat16 [16384, 1280], P(('dp', 'fsdp')), may hold values from -6 to 6
- out_cotangent: bfloat16 [16384, 1280], P(('dp', 'fsdp')), may hold values from -6 to 6
- assignment: int32 [16384, 7], P(('dp', 'fsdp')), may hold values from 0 to 15, all different within a row
- norm_gains: bfloat16 [1280, 2], P(('dp', 'fsdp')), may hold values from 0.5 to 1.5
- attention_weights: bfloat16 [1280, 4, 1280], P(('dp', 'fsdp')), may hold values from -0.67361548 to 0.67361548
- router_weights: bfloat16 [1280, 16], P(('dp', 'fsdp')), may hold values from -0.078125 to 0.078125
- shared_weights: bfloat16 [1280, 3, 896], P(('dp', 'fsdp')), may hold values from -0.15625 to 0.15625
- expert_weights: bfloat16 [16, 3, 1280, 896], P('dp', None, None, 'fsdp'), may hold values from -0.15625 to 0.15625
Outputs:
- block_output: bfloat16 [16384, 1280], P(('dp', 'fsdp'))
- token_gradient: float32 [16384, 1280], P(('dp', 'fsdp'))
- gain_gradient: float32 [1280, 2], P(('dp', 'fsdp'))
- attention_gradient: float32 [1280, 4, 1280], P(('dp', 'fsdp'))
- router_gradient: float32 [1280, 16], P(('dp', 'fsdp'))
- shared_gradient: float32 [1280, 3, 896], P(('dp', 'fsdp'))
- expert_gradient: float32 [16, 3, 1280, 896], P('dp', None, None, 'fsdp')
The draws below stay inside these ranges and needn't reach their ends.
All inputs are finite; a program needn't handle non-finite values.
Results may differ from the reference program's by a relative error of at most 0.014.
Values may be sent and summed in bfloat16 or wider, within the bound.
No kernel may reach another device: no remote copies, remote signals or barrier semaphores. Data moves between devices by JAX's collectives and lax.ppermute only.
A program may use at most 384 MiB of HBM per device.

```python
from functools import partial
import jax
import jax.numpy as jnp
from jax import lax

MODEL_WIDTH = 1280
HEADS = 10
HEAD_SIZE = 128
HIDDEN_SIZE = 896
TOPK = 7
TOK_DEV = 512
EXPERTS = 16
CAP = 192
TOKENS = 16384


def draw_attention_weights(key, part):
    base = jnp.clip(jax.random.normal(key, (MODEL_WIDTH, 4, MODEL_WIDTH), jnp.float32), -3.0, 3.0) * MODEL_WIDTH ** (-0.5)
    factor = jnp.where(jnp.arange(4) == 3, 8.0, 1.0).astype(jnp.float32)
    return (base * factor[None, :, None]).astype(jnp.bfloat16)


def strengthened(array, rng, source, target, parts, factor):
    owner, partner = [(jnp.arange(array.shape[dim]) // (array.shape[dim] // parts)).reshape([-1 if axis == dim else 1 for axis in range(array.ndim)]) for dim in (source, target)]
    chosen = jax.random.permutation(rng, parts)[partner]
    strong = (owner == chosen) | (owner == (partner + parts // 2) % parts)
    return jnp.where(strong, factor * array, array)


def level_of(rng, extent, cuts, least, largest):
    level = 1.0
    for axis_at, shards_of in cuts:
        steps = jax.random.uniform(jax.random.fold_in(jax.random.fold_in(rng, 6), axis_at), (shards_of,), jnp.float32, least / len(cuts), largest / len(cuts))
        level = level * jnp.repeat(jnp.exp(steps), extent[axis_at] // shards_of).reshape((-1,) + (1,) * (len(extent) - 1 - axis_at))
    return level


def picks_of(key, rows, amount, top, lift):
    ranking = jax.random.permutation(jax.random.fold_in(key, 1), amount)
    pull = ranking
    for power in range(3):
        pull = pull * pull // amount
    pull = pull * lift // amount
    chance = jax.random.randint(jax.random.fold_in(key, 2), (rows, amount), 0, 4096) + pull
    fixed_rows = jax.random.permutation(jax.random.fold_in(key, 3), rows)[jnp.arange(amount) % rows]
    chance = jnp.where(jnp.arange(rows)[:, None] == fixed_rows[None, :], 1 << 14, chance)
    score = chance * amount + jnp.arange(amount)
    return lax.top_k(score.astype(jnp.int32), top)[1].astype(jnp.int32)


def normal_values(key, dims, spread, limit, cuts=(), kind=jnp.bfloat16):
    gain = level_of(key, dims, cuts, -0.22, 0.18) if cuts else 1.0
    drawn = jax.random.normal(key, dims, jnp.float32) * spread * gain
    return jnp.minimum(jnp.maximum(drawn, -limit), limit).astype(kind)


def bell_draw_with(stream_key, dims, scale, bound, split, heavy, kind=jnp.bfloat16):
    array = scale * jax.random.normal(stream_key, dims, jnp.float32)
    if split:
        array = array * level_of(stream_key, dims, split, -0.22, 0.18)
    return jnp.clip(strengthened(array, jax.random.fold_in(stream_key, 3), *heavy), -bound, bound).astype(kind)


def setup_inputs(seed: int = 0) -> dict:
    seeds = jax.random.split(jax.random.key(seed), 9)
    return {
        "tokens": bell_draw_with(seeds[0], (TOKENS, MODEL_WIDTH), 1.0, 6.0, ((0, 32),), (0, 1, 32, 2.75)),
        "out_cotangent": normal_values(seeds[1], (TOKENS, MODEL_WIDTH), 1.0, 6.0, ((0, 32),)),
        "assignment": picks_of(seeds[2], TOKENS, EXPERTS, TOPK, 7168),
        "norm_gains": jnp.clip(1.0 + 0.1 * jax.random.normal(seeds[3], (MODEL_WIDTH, 2), jnp.float32), 0.5, 1.5).astype(jnp.bfloat16),
        "attention_weights": draw_attention_weights(jax.random.fold_in(seeds[8], 71), 0),
        "router_weights": normal_values(seeds[5], (MODEL_WIDTH, EXPERTS), (4 * MODEL_WIDTH) ** -0.5, 0.078125, ((0, 32),)),
        "shared_weights": normal_values(seeds[6], (MODEL_WIDTH, 3, HIDDEN_SIZE), MODEL_WIDTH ** -0.5, 0.15625, ((0, 32),)),
        "expert_weights": normal_values(seeds[7], (EXPERTS, 3, MODEL_WIDTH, HIDDEN_SIZE), MODEL_WIDTH ** -0.5, 0.15625, ((0, 8), (3, 4))),
    }


EPSILON = 1e-06
MASKED = -1e+30
TOP_PRECISION = lax.Precision.HIGHEST

@jax.custom_vjp
def low(v):
    return lax.optimization_barrier(v.astype(jnp.bfloat16)).astype(jnp.float32)

@jax.custom_vjp
def low_back(v):
    return v

def low_keep(v):
    return (low(v), None)

def low_pass(kept, grad):
    return (grad,)

def back_keep(v):
    return (v, None)

def back_low(kept, grad):
    return (low(grad),)
low.defvjp(low_keep, low_pass)
low_back.defvjp(back_keep, back_low)

def rotary_tables(sequence_length):
    position = jnp.arange(sequence_length).astype(jnp.float32)
    frequency = 10000.0 ** (-jnp.arange(HEAD_SIZE // 2).astype(jnp.float32) * (2.0 / HEAD_SIZE))
    turned = position[:, None] * frequency[None, :]
    return (jnp.cos(turned)[:, None, :], jnp.sin(turned)[:, None, :])

def rotate(values, cosine_table, sine_table):
    half_size = values.shape[-1] // 2
    first_half = values[..., :half_size]
    second_half = values[..., half_size:]
    return jnp.concatenate([first_half * cosine_table - second_half * sine_table, second_half * cosine_table + first_half * sine_table], axis=-1)

def rms_norm(values, gain_vector):
    inverse_root = lax.rsqrt(lax.optimization_barrier(jnp.mean(values * values, axis=-1, keepdims=True)) + EPSILON)
    return values * inverse_root * gain_vector

def attention_block(normed, attention_weights):
    sequence_length = normed.shape[0]
    projected = jnp.dot(normed, attention_weights[:, :3, :].reshape(MODEL_WIDTH, 3 * MODEL_WIDTH), precision=TOP_PRECISION, preferred_element_type=jnp.float32)
    cosine_table, sine_table = rotary_tables(sequence_length)
    query_rows = low(rotate(low_back(projected[:, :MODEL_WIDTH]).reshape(sequence_length, HEADS, HEAD_SIZE), cosine_table, sine_table))
    rotated_key_rows = low(rotate(low_back(projected[:, MODEL_WIDTH:2 * MODEL_WIDTH]).reshape(sequence_length, HEADS, HEAD_SIZE), cosine_table, sine_table))
    value_rows_full = low(low_back(projected[:, 2 * MODEL_WIDTH:])).reshape(sequence_length, HEADS, HEAD_SIZE)
    score_matrix = jnp.einsum('jus,gus->ujg', query_rows, rotated_key_rows, precision=TOP_PRECISION) * HEAD_SIZE ** (-0.5)
    row_index = jnp.arange(sequence_length)[:, None]
    column_index = jnp.arange(sequence_length)[None, :]
    score_matrix = low_back(jnp.where((row_index >= column_index)[None], score_matrix, MASKED))
    attention_probability = low(jax.nn.softmax(score_matrix, axis=-1))
    blended_value_rows = jnp.einsum('lgv,vlp->glp', attention_probability, value_rows_full, precision=TOP_PRECISION).reshape(sequence_length, MODEL_WIDTH)
    blended_value_rows = low(low_back(blended_value_rows))
    return low_back(jnp.dot(blended_value_rows, attention_weights[:, 3, :], precision=TOP_PRECISION, preferred_element_type=jnp.float32))

def expert_rows(normed_two, weights, token_rows, valid_rows):
    inputs = low_back(normed_two[token_rows] * valid_rows[:, None])
    gate_value = low_back(jnp.dot(inputs, weights[0], precision=TOP_PRECISION, preferred_element_type=jnp.float32))
    up_value = low_back(jnp.dot(inputs, weights[1], precision=TOP_PRECISION, preferred_element_type=jnp.float32))
    hidden = low(jax.nn.silu(gate_value) * up_value)
    return low(low_back(jnp.dot(hidden, weights[2].T, precision=TOP_PRECISION, preferred_element_type=jnp.float32)))

def layer(tables, tokens, norm_gains, attention_weights, router_weights, shared_weights, expert_weights):
    token_table, pair_table, valid_table, chooser = tables
    normed_one = low(rms_norm(tokens, norm_gains[:, 0]))
    sequences = normed_one.reshape(TOKENS // TOK_DEV, TOK_DEV, MODEL_WIDTH)
    attended = lax.map(jax.checkpoint(lambda block: attention_block(block, attention_weights)), sequences)
    hidden_res = tokens + attended.reshape(TOKENS, MODEL_WIDTH)
    normed_two = low(rms_norm(hidden_res, norm_gains[:, 1]))
    shared_gate = low_back(jnp.dot(normed_two, shared_weights[:, 0, :], precision=TOP_PRECISION, preferred_element_type=jnp.float32))
    shared_up = low_back(jnp.dot(normed_two, shared_weights[:, 1, :], precision=TOP_PRECISION, preferred_element_type=jnp.float32))
    shared_hidden = low(jax.nn.silu(shared_gate) * shared_up)
    shared_out = jnp.dot(shared_hidden, shared_weights[:, 2, :].T, precision=TOP_PRECISION, preferred_element_type=jnp.float32)
    logits = low_back(jnp.dot(normed_two, router_weights, precision=TOP_PRECISION, preferred_element_type=jnp.float32))
    router_probability = jax.nn.softmax(logits, axis=-1)
    chosen = lax.optimization_barrier(jnp.sum(chooser * router_probability[:, None, :], axis=-1))
    gates = chosen / lax.optimization_barrier(jnp.sum(chosen, axis=-1, keepdims=True))
    outputs = lax.map(jax.checkpoint(lambda item: expert_rows(normed_two, item[0], item[1], item[2])), (expert_weights, token_table, valid_table))
    slot_gates = gates.reshape(-1)[pair_table] * valid_table
    weighted = outputs * slot_gates[:, :, None]
    routed = jnp.zeros((TOKENS, MODEL_WIDTH), jnp.float32).at[token_table.reshape(-1)].add(weighted.reshape(-1, MODEL_WIDTH))
    return hidden_res + shared_out + routed

def reference(tokens, out_cotangent, assignment, norm_gains, attention_weights, router_weights, shared_weights, expert_weights):
    blocks = TOKENS // TOK_DEV
    pair_count = TOK_DEV * TOPK
    flat_ids = assignment.reshape(blocks, pair_count).astype(jnp.int32)
    expert_range = jnp.arange(EXPERTS).astype(jnp.int32)
    pair_onehot = (flat_ids[:, :, None] == expert_range[None, None, :]).astype(jnp.int32)
    earlier = jnp.cumsum(pair_onehot, axis=1) - pair_onehot
    rank = lax.optimization_barrier(jnp.sum(earlier * pair_onehot, axis=2)).astype(jnp.int32)
    target = jnp.where(rank < CAP, rank, CAP).astype(jnp.int32)
    block_index = jnp.broadcast_to(jnp.arange(blocks).astype(jnp.int32)[:, None], (blocks, pair_count))
    pair_index = (block_index * pair_count + jnp.arange(pair_count).astype(jnp.int32)[None, :]).astype(jnp.int32)
    pair_table = jnp.zeros((EXPERTS, blocks, CAP), jnp.int32).at[flat_ids, block_index, target].set(pair_index, mode='drop').reshape(EXPERTS, blocks * CAP)
    valid_table = jnp.zeros((EXPERTS, blocks, CAP), jnp.float32).at[flat_ids, block_index, target].set(1.0, mode='drop').reshape(EXPERTS, blocks * CAP)
    token_table = (pair_table // TOPK).astype(jnp.int32)
    chooser = (assignment[:, :, None].astype(jnp.int32) == expert_range[None, None, :]).astype(jnp.float32)
    tables = (token_table, pair_table, valid_table, chooser)
    floats = (tokens.astype(jnp.float32), norm_gains.astype(jnp.float32), attention_weights.astype(jnp.float32), router_weights.astype(jnp.float32), shared_weights.astype(jnp.float32), expert_weights.astype(jnp.float32))
    block_output, pullback = jax.vjp(partial(layer, tables), *floats)
    grads = pullback(out_cotangent.astype(jnp.float32))
    return (block_output.astype(jnp.bfloat16), grads[0], grads[1], grads[2], grads[3], grads[4], grads[5])
```

```python
import jax
import jax.numpy as jnp
from jax import lax
from jax.experimental import pallas as pl
from jax.experimental.pallas import tpu as pltpu
from jax.sharding import PartitionSpec as P

HEAD_SIZE = 128
TOPK = 7
EPSILON = 1e-06
MASKED = -1e30
LANES = 128
F32 = jnp.float32
BF16 = jnp.bfloat16
VMEM_LIMIT = 58 * 1024 * 1024


def after(value, *others):
    return lax.optimization_barrier((value, *others))[0]


def core_swap(x):
    return lax.ppermute(x, "dp", [(d, d ^ 1) for d in range(lax.axis_size("dp"))])


def fsdp_swap(x, bit):
    return lax.ppermute(x, "fsdp", [(f, f ^ bit) for f in range(lax.axis_size("fsdp"))])


def line_send(x, step, first, last):
    pairs = [(2 * p + c, 2 * (p + step) + c) for p in range(first, last + 1) for c in range(2)]
    return lax.ppermute(x, "dp", pairs)


def line_gather(x):
    n = lax.axis_size("dp") // 2
    p = lax.axis_index("dp") // 2
    right, left = [x], [x]
    for s in range(1, n):
        a = line_send(right[-1], 1, s - 1, n - 2)
        b = line_send(left[-1], -1, 1, n - s)
        a, b = lax.optimization_barrier((a, b))
        right.append(a)
        left.append(b)
    return [x] + [jnp.where(p + r < n, left[r], right[n - r]) for r in range(1, n)]


def line_scatter(slots, kind=BF16):
    n = len(slots)
    right = left = None
    for s in range(1, n):
        a, b = slots[n - s].astype(F32), slots[s].astype(F32)
        if right is not None:
            a, b = a + right.astype(F32), b + left.astype(F32)
        right = line_send(a.astype(kind), 1, 0, s - 1)
        left = line_send(b.astype(kind), -1, n - s, n - 1)
        right, left = lax.optimization_barrier((right, left))
    total = slots[0].astype(F32)
    return total if right is None else total + right.astype(F32) + left.astype(F32)


def cube_size():
    return max(lax.axis_size("fsdp").bit_length() - 1, 1)


def cube_masks(part):
    k = cube_size()
    masks = [0]
    for j in range(k):
        masks = masks + [m ^ (1 << ((part + j) % k)) for m in masks]
    return masks


def cube_gather(x, part):
    k = cube_size()
    known = [x]
    for j in range(k):
        known = known + [fsdp_swap(a, 1 << ((part + j) % k)) for a in known]
    return known


def cube_scatter(x, part, kind=BF16):
    k = cube_size()
    for j in reversed(range(k)):
        half = x.shape[0] // 2
        got = fsdp_swap(x[half:].astype(kind), 1 << ((part + j) % k))
        x = x[:half].astype(F32) + got.astype(F32)
    return x.astype(F32)


def dense_gather(w):
    slots = line_gather(w)
    own = []
    for part in range(cube_size()):
        own += cube_gather(jnp.concatenate(slots[part :: cube_size()], axis=0), part)
    return own + [core_swap(a) for a in own], slots


def block_order():
    n = lax.axis_size("dp") // 2
    d, f = lax.axis_index("dp"), lax.axis_index("fsdp")
    order = []
    for cx in range(2):
        for part in range(cube_size()):
            for m in cube_masks(part):
                for r in range(n)[part :: cube_size()]:
                    device = ((d // 2 + r) % n) * 2 + (d % 2 ^ cx)
                    order.append(device * lax.axis_size("fsdp") + (f ^ m))
    return jnp.stack(order)


def dense_scatter(own, other, kind=BF16):
    n = lax.axis_size("dp") // 2
    k = cube_size()
    total = own.astype(F32) + core_swap(other.astype(kind)).astype(F32)
    rows = total.shape[0] // (n * 2**k)
    slots = [None] * n
    at = 0
    for part in range(k):
        mine = range(n)[part::k]
        size = 2**k * len(mine) * rows
        got = cube_scatter(total[at : at + size], part, kind)
        at += size
        for i, r in enumerate(mine):
            slots[r] = got[i * rows : (i + 1) * rows]
    return line_scatter(slots, kind)


def token_gather(x):
    return [(a, core_swap(a)) for a in line_gather(x)]


def token_scatter(pairs):
    return line_scatter([a.astype(F32) + core_swap(b).astype(F32) for a, b in pairs])


def dot(a, b, dims):
    return lax.dot_general(a, b, (dims, ((), ())), preferred_element_type=F32)


NN = ((1,), (0,))
NT = ((1,), (1,))
TN = ((0,), (0,))


def turn(x, cosine, sine):
    return x * cosine + pltpu.roll(x, HEAD_SIZE // 2, 1) * sine


def causal_scores(q, k):
    scores = dot(k, q, NT) * (HEAD_SIZE ** (-0.5))
    key = lax.broadcasted_iota(jnp.int32, scores.shape, 0)
    query = lax.broadcasted_iota(jnp.int32, scores.shape, 1)
    return jnp.where(key <= query, scores, MASKED)


def attention_forward_kernel(qp, kp, vp, cosine, sine, q_out, k_out, v_out, mixed_out, lse_out):
    q = turn(qp[...], cosine[...], sine[...]).astype(BF16)
    k = turn(kp[...], cosine[...], sine[...]).astype(BF16)
    v = vp[...].astype(BF16)
    q_out[...] = q
    k_out[...] = k
    v_out[...] = v
    scores = causal_scores(q, k)
    peak = jnp.max(scores, axis=0, keepdims=True)
    expo = jnp.exp(scores - peak)
    totals = jnp.sum(expo, axis=0, keepdims=True)
    lse_out[0] = peak + jnp.log(totals)
    probability = (expo * (1.0 / totals)).astype(BF16)
    mixed_out[...] = dot(probability, v, TN).astype(BF16)


def attention_forward(projected, cosine, sine):
    length = projected.shape[0]
    width = projected.shape[1] // 3
    heads = width // HEAD_SIZE
    block = (length, HEAD_SIZE)
    table = pl.BlockSpec(block, lambda h: (0, 0))
    column = pl.BlockSpec(block, lambda h: (0, h))
    rows = jax.ShapeDtypeStruct((length, width), BF16)
    return pl.pallas_call(
        attention_forward_kernel,
        grid=(heads,),
        in_specs=[
            column,
            pl.BlockSpec(block, lambda h: (0, heads + h)),
            pl.BlockSpec(block, lambda h: (0, 2 * heads + h)),
            table,
            table,
        ],
        out_specs=[column] * 4 + [pl.BlockSpec((1, 1, length), lambda h: (h, 0, 0))],
        out_shape=[rows] * 4 + [jax.ShapeDtypeStruct((heads, 1, length), F32)],
        compiler_params=pltpu.CompilerParams(vmem_limit_bytes=VMEM_LIMIT),
        name="attention_forward",
    )(projected, projected, projected, cosine, sine)


def attention_backward_kernel(q_in, k_in, v_in, d_in, lse, cosine, sine, dq_out, dk_out, dv_out):
    q, k, v, d = q_in[...], k_in[...], v_in[...], d_in[...]
    scale = HEAD_SIZE ** (-0.5)
    probability = jnp.exp(causal_scores(q, k) - lse[0])
    dv_out[...] = dot(probability.astype(BF16), d, NN).astype(BF16)
    prob_cot = dot(v, d, NT)
    row_dot = jnp.sum(probability * prob_cot, axis=0, keepdims=True)
    score_cot = (probability * (prob_cot - row_dot)).astype(BF16)
    dk = dot(score_cot, q, NN) * scale
    dq = dot(score_cot, k, TN) * scale
    dq_out[...] = turn(dq, cosine[...], -sine[...]).astype(BF16)
    dk_out[...] = turn(dk, cosine[...], -sine[...]).astype(BF16)


def attention_backward(q, k, v, mixed_cot, lse, cosine, sine):
    length, width = q.shape
    heads = width // HEAD_SIZE
    block = (length, HEAD_SIZE)
    table = pl.BlockSpec(block, lambda h: (0, 0))
    column = pl.BlockSpec(block, lambda h: (0, h))
    return pl.pallas_call(
        attention_backward_kernel,
        grid=(heads,),
        in_specs=[column] * 4
        + [pl.BlockSpec((1, 1, length), lambda h: (h, 0, 0)), table, table],
        out_specs=[column] * 3,
        out_shape=[jax.ShapeDtypeStruct((length, width), BF16)] * 3,
        compiler_params=pltpu.CompilerParams(vmem_limit_bytes=VMEM_LIMIT),
        name="attention_backward",
    )(q, k, v, mixed_cot, lse, cosine, sine)


def silu_parts(gate_value):
    sigmoid_value = jax.nn.sigmoid(gate_value)
    return (gate_value * sigmoid_value, sigmoid_value * (1.0 + gate_value * (1.0 - sigmoid_value)))


def expert_kernel(
    first, x_own, x_other, c_own, c_other, router, weights,
    x_out, c_out, h_out, g_out, u_out, cot_own, cot_other, out_own, out_other, router_out,
    cot_scratch, out_scratch, router_scratch,
):
    length, width = x_own.shape
    capacity = x_out.shape[1] // 2
    experts = router.shape[0]
    local = pl.num_programs(0)
    step = pl.program_id(0)
    sources = ((x_own, c_own), (x_other, c_other))

    @pl.when(step == 0)
    def _():
        cot_scratch[...] = jnp.zeros_like(cot_scratch)
        out_scratch[...] = jnp.zeros_like(out_scratch)
        router_scratch[...] = jnp.zeros_like(router_scratch)

    wanted = first[0] + step
    expert_row = lax.broadcasted_iota(jnp.int32, (experts, length), 0)
    slot_row = lax.broadcasted_iota(jnp.int32, (capacity, length), 0).astype(F32)
    picks, gate_columns, tables = [], [], []
    for at, (x_ref, c_ref) in enumerate(sources):
        x = x_ref[...]
        ranks = c_ref[length : length + experts, :length].astype(F32)
        rank = jnp.sum(jnp.where(expert_row == wanted, ranks, 0.0), axis=0, keepdims=True)
        pick = jnp.where(slot_row == rank, 1.0, 0.0)
        logits = dot(router[...], x, NT)
        expo = jnp.exp(logits - jnp.max(logits, axis=0, keepdims=True))
        probability = expo * (1.0 / jnp.sum(expo, axis=0, keepdims=True))
        chosen = jnp.where(ranks >= 0.0, probability, 0.0)
        chosen_total = jnp.sum(chosen, axis=0, keepdims=True)
        mine = jnp.sum(jnp.where(expert_row == wanted, chosen, 0.0), axis=0, keepdims=True)
        gate = mine / chosen_total
        gate_columns.append(jnp.sum(pick * gate, axis=1, keepdims=True))
        pick16 = pick.astype(BF16)
        picks.append(pick16)
        tables.append((ranks, probability, chosen, chosen_total, mine))
        low, high = at * capacity, (at + 1) * capacity
        x_out[0, low:high, :] = dot(pick16, x, NN).astype(BF16)
        c_out[0, low:high, :] = dot(pick16, c_ref[:length, :], NN).astype(BF16)
    gates = jnp.concatenate(gate_columns, axis=0)
    x = x_out[0]
    c = c_out[0]
    gate_value = dot(x, weights[0, 0], NT)
    up_value = dot(x, weights[0, 1], NT)
    active, slope = silu_parts(gate_value)
    hidden = active * up_value
    raw_cot = dot(c, weights[0, 2], NT)
    hidden16 = hidden.astype(BF16)
    gate_cot = jnp.sum(raw_cot * hidden16.astype(F32), axis=1, keepdims=True)
    hidden_cot = gates * raw_cot
    h_out[0] = hidden16
    g16 = (hidden_cot * up_value * slope).astype(BF16)
    u16 = (hidden_cot * active).astype(BF16)
    g_out[0] = g16
    u_out[0] = u16
    c_out[0] = (gates * c.astype(F32)).astype(BF16)
    x_cot = (dot(g16, weights[0, 0], NN) + dot(u16, weights[0, 1], NN)).astype(BF16)
    y = dot((gates * hidden16.astype(F32)).astype(BF16), weights[0, 2], NN).astype(BF16)
    for at, (x_ref, _) in enumerate(sources):
        low, high = at * capacity, (at + 1) * capacity
        ranks, probability, chosen, chosen_total, mine = tables[at]
        back = jnp.sum(picks[at].astype(F32) * gate_cot[low:high], axis=0, keepdims=True)
        shift = back * mine / (chosen_total * chosen_total)
        direct = jnp.where(expert_row == wanted, back / chosen_total, 0.0)
        prob_cot = jnp.where(ranks >= 0.0, direct - shift, 0.0)
        inner = jnp.sum(prob_cot * probability, axis=0, keepdims=True)
        logit_cot = (probability * (prob_cot - inner)).astype(BF16)
        cot_scratch[at] += dot(picks[at], x_cot[low:high], TN) + dot(logit_cot, router[...], TN)
        out_scratch[at] += dot(picks[at], y[low:high], TN)
        router_scratch[...] += dot(logit_cot, x_ref[...], NN)

    @pl.when(step == local - 1)
    def _():
        cot_own[...] = cot_scratch[0].astype(BF16)
        cot_other[...] = cot_scratch[1].astype(BF16)
        out_own[...] = out_scratch[0].astype(BF16)
        out_other[...] = out_scratch[1].astype(BF16)
        router_out[...] = router_scratch[...]


def expert_chunk(first, x_pair, c_pair, router, weights, capacity):
    length, width = x_pair[0].shape
    local, _, units, _ = weights.shape
    experts = router.shape[0]
    whole = lambda shape: pl.BlockSpec(shape, lambda e, s: (0,) * len(shape))
    per = lambda shape: pl.BlockSpec((1,) + shape, lambda e, s: (e,) + (0,) * len(shape))
    slots = 2 * capacity
    shape = jax.ShapeDtypeStruct
    return pl.pallas_call(
        expert_kernel,
        grid_spec=pltpu.PrefetchScalarGridSpec(
            num_scalar_prefetch=1,
            grid=(local,),
            in_specs=[
                whole((length, width)),
                whole((length, width)),
                whole(c_pair[0].shape),
                whole(c_pair[1].shape),
                whole((experts, width)),
                per((3, units, width)),
            ],
            out_specs=[per((slots, width))] * 2
            + [per((slots, units))] * 3
            + [whole((length, width))] * 4
            + [whole((experts, width))],
            scratch_shapes=[
                pltpu.VMEM((2, length, width), F32),
                pltpu.VMEM((2, length, width), F32),
                pltpu.VMEM((experts, width), F32),
            ],
        ),
        out_shape=[shape((local, slots, width), BF16)] * 2
        + [shape((local, slots, units), BF16)] * 3
        + [shape((length, width), BF16)] * 4
        + [shape((experts, width), F32)],
        compiler_params=pltpu.CompilerParams(vmem_limit_bytes=VMEM_LIMIT),
        name="expert_chunk",
    )(first, *x_pair, *c_pair, router, weights)


def expert_weights_kernel(*refs):
    *inputs, out = refs
    n = len(inputs) // 2
    total = None
    for left, right in zip(inputs[:n], inputs[n:]):
        part = dot(left[0], right[0], TN)
        total = part if total is None else total + part
    out[0] = total.astype(BF16)


def expert_weight_part(left, right):
    local, slots, units = left[0].shape
    width = right[0].shape[2]
    return pl.pallas_call(
        expert_weights_kernel,
        grid=(local,),
        in_specs=[pl.BlockSpec((1, slots, units), lambda e: (e, 0, 0))] * len(left)
        + [pl.BlockSpec((1, slots, width), lambda e: (e, 0, 0))] * len(right),
        out_specs=pl.BlockSpec((1, units, width), lambda e: (e, 0, 0)),
        out_shape=jax.ShapeDtypeStruct((local, units, width), BF16),
        compiler_params=pltpu.CompilerParams(vmem_limit_bytes=VMEM_LIMIT),
        name="expert_weights",
    )(*left, *right)


def split_matmul(values, matrix, dims):
    high = values.astype(BF16)
    low = (values - high.astype(F32)).astype(BF16)
    return dot(high, matrix, dims) + dot(low, matrix, dims)


def exact_matmul(values, matrix, dims):
    return lax.dot_general(
        values, matrix.astype(F32), (dims, ((), ())),
        precision=lax.Precision.HIGHEST, preferred_element_type=F32,
    )


def shards(
    tokens,
    out_cotangent,
    assignment,
    norm_gains,
    attention_weights,
    router_weights,
    shared_weights,
    expert_weights,
):
    length, width = tokens.shape
    rows = attention_weights.shape[0]
    ranks = lax.axis_size("dp")
    local = expert_weights.shape[0]
    experts = local * ranks
    capacity = length * 6 // experts
    units = shared_weights.shape[2]
    n = ranks // 2

    small = jnp.concatenate([norm_gains, router_weights], axis=1)
    small = jnp.pad(small, ((0, 0), (0, LANES - small.shape[1])))
    packed = jnp.concatenate([attention_weights[:, :3].reshape(rows, 3 * width), small], axis=1)
    pieces, line = dense_gather(packed)
    project = jnp.concatenate([a[:, : 3 * width] for a in pieces], axis=0)
    small_full = jnp.concatenate([a[:, 3 * width :] for a in pieces], axis=0)
    out_local, shared_local = attention_weights[:, 3], shared_weights.reshape(rows, 3 * units)
    out_local = after(out_local, *line)
    pieces, line = dense_gather(out_local)
    out_full = jnp.concatenate(pieces, axis=0)
    shared_local = after(shared_local, *line)
    pieces, line = dense_gather(shared_local)
    shared_full = jnp.concatenate(pieces, axis=0)
    shared_gu, shared_down = shared_full[:, : 2 * units], shared_full[:, 2 * units :]

    turned = jnp.transpose(expert_weights, (0, 1, 3, 2))
    routed = [
        jnp.concatenate(cube_gather(turned[e], e % cube_size()), axis=1) for e in range(local)
    ]
    routed = jnp.stack(routed)

    hot = jnp.sum(
        (assignment[:, :, None] == jnp.arange(experts)[None, None, :]).astype(F32), axis=1
    )
    before = (jnp.arange(length)[:, None] < jnp.arange(length)[None, :]).astype(BF16)
    earlier = dot(hot.astype(BF16), before, TN)
    places = jnp.where(hot.T > 0, jnp.minimum(earlier, float(capacity)), -1.0).astype(BF16)
    places = jnp.pad(places, ((0, 0), (0, width - length)))
    sent = jnp.concatenate([out_cotangent, places], axis=0)
    c_pairs = token_gather(after(sent, *line))

    owner = block_order()
    true_row = (owner[:, None] * rows + jnp.arange(rows)[None, :]).reshape(width)
    order = (jnp.arange(width)[:, None] == true_row[None, :]).astype(BF16)
    tokens_float = tokens.astype(F32)
    tokens_rel = dot(tokens, order, NN)
    c_rel = dot(out_cotangent, order, NN).astype(BF16)
    root_one = lax.rsqrt(jnp.mean(tokens_float * tokens_float, axis=-1, keepdims=True) + EPSILON)
    position = jnp.arange(length).astype(F32)
    frequency = 10000.0 ** (-jnp.arange(HEAD_SIZE // 2).astype(F32) * (2.0 / HEAD_SIZE))
    angle = position[:, None] * frequency[None, :]
    cosine = jnp.concatenate([jnp.cos(angle), jnp.cos(angle)], axis=1)
    sine = jnp.concatenate([-jnp.sin(angle), jnp.sin(angle)], axis=1)

    small_true = dot(order, small_full, NN)
    gain_one = small_full[:, 0].astype(F32)
    gain_two = small_true[:, 1]
    router = small_true[:, 2 : 2 + experts].T.astype(BF16)

    unit_one = tokens_rel * root_one
    normed_one = (unit_one * gain_one).astype(BF16)
    projected = dot(normed_one, project, NN)
    query, key, value, mixed, lse = attention_forward(projected, cosine, sine)
    mixed_rel = dot(mixed, order, NN).astype(BF16)
    hidden_res = tokens_float + dot(mixed_rel, out_full, NN)
    root_two = lax.rsqrt(jnp.mean(hidden_res * hidden_res, axis=-1, keepdims=True) + EPSILON)
    unit_two = hidden_res * root_two
    normed_two = (unit_two * gain_two).astype(BF16)
    x_pairs = token_gather(normed_two)

    normed_rel = dot(normed_two, order, NN).astype(BF16)
    gate_up = dot(normed_rel, shared_gu, NN)
    shared_active, shared_slope = silu_parts(gate_up[:, :units])
    shared_up = gate_up[:, units:]
    shared_hidden = (shared_active * shared_up).astype(BF16)
    shared_out = split_matmul(dot(shared_hidden, shared_down, NT), order, NT)
    shared_cot = dot(c_rel, shared_down, NN)
    gate_up_cot = jnp.concatenate(
        [
            (shared_cot * shared_up * shared_slope).astype(BF16),
            (shared_cot * shared_active).astype(BF16),
        ],
        axis=1,
    )
    half = width // 2
    shared_grad = [
        jnp.concatenate(
            [dot(normed_rel[:, cut], gate_up_cot, TN).astype(BF16),
             dot(c_rel[:, cut], shared_hidden, TN).astype(BF16)], axis=1,
        )
        for cut in (slice(0, half), slice(half, width))
    ]
    shared_back = split_matmul(dot(gate_up_cot, shared_gu, NT), order, NT)

    first = (lax.axis_index("dp") * local).astype(jnp.int32).reshape(1)
    done = {}
    for r in [0] + [r for i in range(n // 2, 0, -1) for r in sorted({i, n - i}) if 0 < r < n]:
        done[r] = expert_chunk(first, x_pairs[r], c_pairs[r], router, routed, capacity)
    chunks = [done[r] for r in range(n)]
    back_sum = token_scatter([(a[5], a[6]) for a in chunks])
    router_part = sum(a[9] for a in chunks)
    expert_grads = [
        expert_weight_part([a[i] for a in chunks], [a[j] for a in chunks])
        for i, j in ((3, 0), (4, 0), (2, 1))
    ]
    out_pairs = lax.optimization_barrier(([(a[7], a[8]) for a in chunks], back_sum))[0]
    out_sum = token_scatter(out_pairs)
    block_output = (hidden_res + shared_out + out_sum).astype(BF16)
    expert_gradient = jnp.stack(
        [
            jnp.stack([cube_scatter(g[e], e % cube_size()).T for g in expert_grads])
            for e in range(local)
        ]
    )

    cotangent = out_cotangent.astype(F32)
    normed_two_cot = back_sum + shared_back
    scaled = normed_two_cot * gain_two
    gain_two_grad = jnp.sum(normed_two_cot * unit_two, axis=0)
    hidden_cot = cotangent + root_two * (
        scaled - unit_two * jnp.mean(scaled * unit_two, axis=-1, keepdims=True)
    )
    attn_cot = hidden_cot.astype(BF16)
    mixed_cot = dot(dot(attn_cot, out_full, NT).astype(BF16), order, NT).astype(BF16)
    out_grad = [dot(mixed_rel[:, cut], attn_cot, TN).astype(BF16)
                for cut in (slice(0, half), slice(half, width))]
    cots = attention_backward(query, key, value, mixed_cot, lse, cosine, sine)
    projected_cot = jnp.concatenate(cots, axis=1)
    in_grad = [dot(normed_one[:, cut], projected_cot, TN).astype(BF16)
               for cut in (slice(0, half), slice(half, width))]
    normed_one_cot = dot(projected_cot, project, NT)
    scaled_one = normed_one_cot * gain_one
    gain_one_grad = jnp.sum(normed_one_cot * unit_one, axis=0)
    token_part = root_one * (
        scaled_one - unit_one * jnp.mean(scaled_one * unit_one, axis=-1, keepdims=True)
    )
    token_gradient = hidden_cot + split_matmul(token_part, order, NT)

    shared_gradient = dense_scatter(*shared_grad).reshape(rows, 3, units)
    out_gradient = dense_scatter(*out_grad)
    in_gradient = dense_scatter(*in_grad).reshape(rows, 3, width)
    attention_gradient = jnp.concatenate([in_gradient, out_gradient[:, None, :]], axis=1)
    true_part = exact_matmul(
        jnp.concatenate([gain_two_grad[None, :], router_part], axis=0), order, NN
    )
    small_grad = jnp.concatenate([gain_one_grad[None, :], true_part], axis=0)
    small_grad = jnp.pad(small_grad, ((0, LANES - small_grad.shape[0]), (0, 0))).T
    small_gradient = dense_scatter(small_grad[:half], small_grad[half:], F32)
    return (
        block_output,
        token_gradient,
        small_gradient[:, :2],
        attention_gradient,
        small_gradient[:, 2 : 2 + experts],
        shared_gradient,
        expert_gradient,
    )


def solution(mesh):
    both = ("dp", "fsdp")
    return jax.shard_map(
        shards,
        mesh=mesh,
        in_specs=(
            P(both, None),
            P(both, None),
            P(both, None),
            P(both, None),
            P(both, None, None),
            P(both, None),
            P(both, None, None),
            P("dp", None, None, "fsdp"),
        ),
        out_specs=(
            P(both, None),
            P(both, None),
            P(both, None),
            P(both, None, None),
            P(both, None),
            P(both, None, None),
            P("dp", None, None, "fsdp"),
        ),
        check_vma=False,
    )
```

```python
import jax
import jax.numpy as jnp
from jax import lax
from jax.experimental import pallas as pl
from jax.experimental.pallas import tpu as pltpu
from jax.sharding import PartitionSpec as P

HEAD_SIZE = 128
TOPK = 7
EPSILON = 1e-06
MASKED = -1e30
LANES = 128
F32 = jnp.float32
BF16 = jnp.bfloat16
VMEM_LIMIT = 58 * 1024 * 1024


def after(values, *others):
    return lax.optimization_barrier((values, others))[0]


def core_swap(x):
    return lax.ppermute(x, "dp", [(d, d ^ 1) for d in range(lax.axis_size("dp"))])


def fsdp_swap(x, bit):
    return lax.ppermute(x, "fsdp", [(f, f ^ bit) for f in range(lax.axis_size("fsdp"))])


def positions():
    return lax.axis_size("dp") // 2


def line_fetch(x):
    n = positions()
    pairs = lambda r: [
        (2 * ((p + r) % n) + c, 2 * p + c) for p in range(n) for c in range(2)
    ]
    return [x] + [lax.ppermute(x, "dp", pairs(r)) for r in range(1, n)]


def line_return(slots, kind=BF16):
    n = positions()
    pairs = lambda r: [
        (2 * p + c, 2 * ((p + r) % n) + c) for p in range(n) for c in range(2)
    ]
    return [slots[0]] + [lax.ppermute(slots[r].astype(kind), "dp", pairs(r)) for r in range(1, n)]


def add_all(parts):
    return sum(a.astype(F32) for a in parts)


def line_send(x, step, first, last):
    pairs = [(2 * p + c, 2 * (p + step) + c) for p in range(first, last + 1) for c in range(2)]
    return lax.ppermute(x, "dp", pairs)


class LineGather:
    def __init__(self, x):
        self.right, self.left = [x], [x]
        self.n = positions()

    def step(self, *others):
        s = len(self.right)
        a, b = after((self.right[-1], self.left[-1]), *others)
        self.right.append(line_send(a, 1, s - 1, self.n - 2))
        self.left.append(line_send(b, -1, 1, self.n - s))
        return self.right[-1], self.left[-1]

    def slot(self, r):
        if r == 0:
            return self.right[0]
        p = lax.axis_index("dp") // 2
        return jnp.where(p + r < self.n, self.left[r], self.right[self.n - r])


class LineScatter:
    def __init__(self):
        self.right = self.left = None
        self.s = 0
        self.n = positions()

    def step(self, to_right, to_left, *others):
        self.s += 1
        s = self.s
        a, b = to_right.astype(F32), to_left.astype(F32)
        if self.right is not None:
            a, b = a + self.right.astype(F32), b + self.left.astype(F32)
        a, b = after((a.astype(BF16), b.astype(BF16)), *others)
        self.sent = a, b
        self.right = line_send(a, 1, 0, s - 1)
        self.left = line_send(b, -1, self.n - s, self.n - 1)
        return self.right, self.left

    def total(self, own):
        if self.right is None:
            return own.astype(F32)
        return own.astype(F32) + self.right.astype(F32) + self.left.astype(F32)


def cube_size():
    return max(lax.axis_size("fsdp").bit_length() - 1, 1)


def cube_bit(part, j):
    return 1 << ((part + j) % cube_size())


def cube_masks(part):
    masks = [0]
    for j in range(cube_size()):
        masks = masks + [m ^ cube_bit(part, j) for m in masks]
    return masks


def add_pair(pair):
    return pair[0].astype(F32) + pair[1].astype(F32)


def dense_parts(slots):
    k = cube_size()
    return [jnp.concatenate(slots[part::k], axis=0) for part in range(k)]


class DenseGather:
    def __init__(self, slots):
        self.held = dense_parts(slots)
        self.j = 0

    def exchange(self, *others):
        self.held = after(self.held, *others)
        self.got = [fsdp_swap(a, cube_bit(part, self.j)) for part, a in enumerate(self.held)]
        self.j += 1
        return self.got

    def join(self):
        self.held = [jnp.concatenate(pair, axis=0) for pair in zip(self.held, self.got)]

    def swap_held(self, *others):
        self.first = core_swap(after(jnp.concatenate(self.held, axis=0), *others))
        return self.first

    def swap_got(self, *others):
        self.second = core_swap(after(jnp.concatenate(self.got, axis=0), *others))
        return self.second

    def swap_all(self, *others):
        both = jnp.concatenate(self.held + self.got, axis=0)
        both = core_swap(after(both, *others))
        size = sum(a.shape[0] for a in self.held)
        self.first, self.second = both[:size], both[size:]
        return both

    def pieces(self):
        own, other, at = [], [], 0
        for a, b in zip(self.held, self.got):
            size = a.shape[0]
            own += [a, b]
            other += [self.first[at : at + size], self.second[at : at + size]]
            at += size
        return own + other

    def columns(self, start, stop):
        return jnp.concatenate([a[:, start:stop] for a in self.pieces()], axis=0)


def block_order():
    n = positions()
    d, f = lax.axis_index("dp"), lax.axis_index("fsdp")
    order = []
    for cx in range(2):
        for part in range(cube_size()):
            for m in cube_masks(part):
                for r in range(n)[part :: cube_size()]:
                    device = ((d // 2 + r) % n) * 2 + (d % 2 ^ cx)
                    order.append(device * lax.axis_size("fsdp") + (f ^ m))
    return jnp.stack(order)


class DenseScatter:
    def __init__(self, own, other, kind=BF16):
        self.own, self.other, self.kind = own, other, kind

    def swap(self, *others):
        other = after(self.other.astype(self.kind), *others)
        self.got = core_swap(other)
        return self.got

    def cut(self, extra):
        total = add_pair((self.own, self.got))
        if extra is not None:
            total = jnp.concatenate([total, add_pair((extra.own, extra.got))], axis=1)
        n, k = positions(), cube_size()
        rows = total.shape[0] // (n * 2**k)
        self.parts, at = [], 0
        for part in range(k):
            size = 2**k * len(range(n)[part::k]) * rows
            self.parts.append(total[at : at + size])
            at += size
        self.rows = rows

    def exchange(self, i, *others, extra=None):
        j = cube_size() - 1 - i
        if i > 0:
            self.parts = [add_pair(pair) for pair in self.pairs]
        else:
            self.cut(extra)
        halves = [x.shape[0] // 2 for x in self.parts]
        sent = after([x[h:].astype(self.kind) for x, h in zip(self.parts, halves)], *others)
        self.pairs = [
            (x[:h], fsdp_swap(y, cube_bit(part, j)))
            for part, (x, y, h) in enumerate(zip(self.parts, sent, halves))
        ]
        return [b for _, b in self.pairs]

    def line(self, *others):
        n, k = positions(), cube_size()
        slots = [None] * n
        for part, pair in enumerate(self.pairs):
            got = add_pair(pair)
            for i, r in enumerate(range(n)[part::k]):
                slots[r] = got[i * self.rows : (i + 1) * self.rows]
        sent = after([x.astype(self.kind) for x in slots[1:]], *others)
        self.arrived = line_return([slots[0]] + sent, self.kind)
        return self.arrived[1:]

    def total(self):
        return add_all(self.arrived)


def dot(a, b, dims):
    return lax.dot_general(a, b, (dims, ((), ())), preferred_element_type=F32)


NN = ((1,), (0,))
NT = ((1,), (1,))
TN = ((0,), (0,))


def turn(x, cosine, sine):
    return x * cosine + pltpu.roll(x, HEAD_SIZE // 2, 1) * sine


def causal_scores(q, k):
    scores = dot(k, q, NT) * (HEAD_SIZE ** (-0.5))
    key = lax.broadcasted_iota(jnp.int32, scores.shape, 0)
    query = lax.broadcasted_iota(jnp.int32, scores.shape, 1)
    return jnp.where(key <= query, scores, MASKED)


def cost(flops, transcendentals=0):
    return pl.CostEstimate(
        flops=int(flops), transcendentals=int(transcendentals), bytes_accessed=int(flops // 400)
    )


def attention_forward_kernel(qp, kp, vp, cosine, sine, q_out, k_out, v_out, mixed_out, lse_out):
    q = turn(qp[...], cosine[...], sine[...]).astype(BF16)
    k = turn(kp[...], cosine[...], sine[...]).astype(BF16)
    v = vp[...].astype(BF16)
    q_out[...] = q
    k_out[...] = k
    v_out[...] = v
    scores = causal_scores(q, k)
    peak = jnp.max(scores, axis=0, keepdims=True)
    expo = jnp.exp(scores - peak)
    totals = jnp.sum(expo, axis=0, keepdims=True)
    lse_out[0] = peak + jnp.log(totals)
    probability = (expo * (1.0 / totals)).astype(BF16)
    mixed_out[...] = dot(probability, v, TN).astype(BF16)


def attention_forward(projected, cosine, sine):
    length = projected.shape[0]
    width = projected.shape[1] // 3
    heads = width // HEAD_SIZE
    block = (length, HEAD_SIZE)
    table = pl.BlockSpec(block, lambda h: (0, 0))
    column = pl.BlockSpec(block, lambda h: (0, h))
    rows = jax.ShapeDtypeStruct((length, width), BF16)
    return pl.pallas_call(
        attention_forward_kernel,
        grid=(heads,),
        in_specs=[
            column,
            pl.BlockSpec(block, lambda h: (0, heads + h)),
            pl.BlockSpec(block, lambda h: (0, 2 * heads + h)),
            table,
            table,
        ],
        out_specs=[column] * 4 + [pl.BlockSpec((1, 1, length), lambda h: (h, 0, 0))],
        out_shape=[rows] * 4 + [jax.ShapeDtypeStruct((heads, 1, length), F32)],
        compiler_params=pltpu.CompilerParams(vmem_limit_bytes=VMEM_LIMIT),
        cost_estimate=cost(14e9),
        name="attention_forward",
    )(projected, projected, projected, cosine, sine)


def attention_backward_kernel(q_in, k_in, v_in, d_in, lse, cosine, sine, dq_out, dk_out, dv_out):
    q, k, v, d = q_in[...], k_in[...], v_in[...], d_in[...]
    scale = HEAD_SIZE ** (-0.5)
    probability = jnp.exp(causal_scores(q, k) - lse[0])
    dv_out[...] = dot(probability.astype(BF16), d, NN).astype(BF16)
    prob_cot = dot(v, d, NT)
    row_dot = jnp.sum(probability * prob_cot, axis=0, keepdims=True)
    score_cot = (probability * (prob_cot - row_dot)).astype(BF16)
    dk = dot(score_cot, q, NN) * scale
    dq = dot(score_cot, k, TN) * scale
    dq_out[...] = turn(dq, cosine[...], -sine[...]).astype(BF16)
    dk_out[...] = turn(dk, cosine[...], -sine[...]).astype(BF16)


def attention_backward(q, k, v, mixed_cot, lse, cosine, sine):
    length, width = q.shape
    heads = width // HEAD_SIZE
    block = (length, HEAD_SIZE)
    table = pl.BlockSpec(block, lambda h: (0, 0))
    column = pl.BlockSpec(block, lambda h: (0, h))
    return pl.pallas_call(
        attention_backward_kernel,
        grid=(heads,),
        in_specs=[column] * 4
        + [pl.BlockSpec((1, 1, length), lambda h: (h, 0, 0)), table, table],
        out_specs=[column] * 3,
        out_shape=[jax.ShapeDtypeStruct((length, width), BF16)] * 3,
        compiler_params=pltpu.CompilerParams(vmem_limit_bytes=VMEM_LIMIT),
        cost_estimate=cost(15e9),
        name="attention_backward",
    )(q, k, v, mixed_cot, lse, cosine, sine)


def silu_parts(gate_value):
    sigmoid_value = jax.nn.sigmoid(gate_value)
    return (gate_value * sigmoid_value, sigmoid_value * (1.0 + gate_value * (1.0 - sigmoid_value)))


def expert_kernel(
    first, x_own, x_other, c_own, c_other, router, weights,
    x_out, c_out, h_out, g_out, u_out, cot_own, cot_other, out_own, out_other, router_out,
    picks, xs, cs, x_cots, ys, shares, backs,
):
    length, width = x_own.shape
    capacity = x_out.shape[1] // 2
    experts = router.shape[0]
    local = pl.num_programs(0)
    count = picks.shape[1] // capacity
    step = pl.program_id(0)
    sources = ((x_own, c_own), (x_other, c_other))
    w_gate, w_up, w_down = (weights[:, 0, i].reshape(-1, width) for i in range(3))
    expert_row = lax.broadcasted_iota(jnp.int32, (experts, length), 0)
    slot_row = lax.broadcasted_iota(jnp.int32, (capacity, length), 0).astype(F32)

    def row_of(table, index):
        return jnp.sum(jnp.where(expert_row == index, table, 0.0), axis=0, keepdims=True)

    @pl.when(step == 0)
    def _():
        for at, (x_ref, c_ref) in enumerate(sources):
            ranks = c_ref[length : length + experts, :length].astype(F32)
            logits = dot(router[...], x_ref[...], NT)
            expo = jnp.exp(logits - jnp.max(logits, axis=0, keepdims=True))
            shares[at] = expo * (1.0 / jnp.sum(expo, axis=0, keepdims=True))
            pick = jnp.concatenate(
                [jnp.where(slot_row == row_of(ranks, first[0] + e), 1.0, 0.0) for e in range(count)],
                axis=0,
            ).astype(BF16)
            picks[at] = pick
            x = dot(pick, x_ref[...], NN).astype(BF16)
            c = dot(pick, c_ref[:length, :], NN).astype(BF16)
            for e in range(count):
                low, high = e * capacity, (e + 1) * capacity
                xs[e, at * capacity : (at + 1) * capacity, :] = x[low:high]
                cs[e, at * capacity : (at + 1) * capacity, :] = c[low:high]

    x = xs[step]
    c = cs[step]
    gate_columns = []
    for at, (_, c_ref) in enumerate(sources):
        ranks = c_ref[length : length + experts, :length].astype(F32)
        chosen = jnp.where(ranks >= 0.0, shares[at], 0.0)
        gate = row_of(chosen, first[0] + step) / jnp.sum(chosen, axis=0, keepdims=True)
        pick = picks[at, pl.ds(pl.multiple_of(step * capacity, 32), capacity), :].astype(F32)
        gate_columns.append(jnp.sum(pick * gate, axis=1, keepdims=True))
    gates = jnp.concatenate(gate_columns, axis=0)
    x_out[0] = x
    c_out[0] = (gates * c.astype(F32)).astype(BF16)
    gate_value = dot(x, w_gate, NT)
    up_value = dot(x, w_up, NT)
    raw_cot = dot(c, w_down, NT)
    active, slope = silu_parts(gate_value)
    hidden16 = (active * up_value).astype(BF16)
    hidden = hidden16.astype(F32)
    gate_cot = jnp.sum(raw_cot * hidden, axis=1, keepdims=True)
    hidden_cot = gates * raw_cot
    h_out[0] = hidden16
    g16 = (hidden_cot * up_value * slope).astype(BF16)
    u16 = (hidden_cot * active).astype(BF16)
    g_out[0] = g16
    u_out[0] = u16
    x_cot = (dot(g16, w_gate, NN) + dot(u16, w_up, NN)).astype(BF16)
    y = dot((gates * hidden).astype(BF16), w_down, NN).astype(BF16)
    for at in range(2):
        low, high = at * capacity, (at + 1) * capacity
        rows = pl.ds(pl.multiple_of(step * capacity, 32), capacity)
        x_cots[at, rows, :] = x_cot[low:high]
        ys[at, rows, :] = y[low:high]
        pick = picks[at, rows, :].astype(F32)
        backs[at, step] = jnp.sum(pick * gate_cot[low:high], axis=0, keepdims=True)

    @pl.when(step == local - 1)
    def _():
        for at, (x_ref, c_ref) in enumerate(sources):
            ranks = c_ref[length : length + experts, :length].astype(F32)
            probability = shares[at]
            chosen = jnp.where(ranks >= 0.0, probability, 0.0)
            total = jnp.sum(chosen, axis=0, keepdims=True)
            direct = jnp.zeros_like(chosen)
            shift = jnp.zeros_like(total)
            for e in range(count):
                back = backs[at, e]
                shift += back * row_of(chosen, first[0] + e)
                direct += jnp.where(expert_row == first[0] + e, back / total, 0.0)
            prob_cot = jnp.where(ranks >= 0.0, direct - shift / (total * total), 0.0)
            inner = jnp.sum(prob_cot * probability, axis=0, keepdims=True)
            logit_cot = (probability * (prob_cot - inner)).astype(BF16)
            cot = dot(picks[at], x_cots[at], TN) + dot(logit_cot, router[...], TN)
            out = dot(picks[at], ys[at], TN)
            (cot_own, cot_other)[at][...] = cot.astype(BF16)
            (out_own, out_other)[at][...] = out.astype(BF16)
            part = dot(logit_cot, x_ref[...], NN)
            router_out[...] = part if at == 0 else router_out[...] + part


def expert_chunk(first, x_pair, c_pair, router, weights, capacity):
    length, width = x_pair[0].shape
    pieces, local, _, part, _ = weights.shape
    units = pieces * part
    experts = router.shape[0]
    whole = lambda shape: pl.BlockSpec(
        shape, lambda e, s: (0,) * len(shape), pipeline_mode=pl.Buffered(1)
    )
    per = lambda shape: pl.BlockSpec((1,) + shape, lambda e, s: (e,) + (0,) * len(shape))
    slots = 2 * capacity
    shape = jax.ShapeDtypeStruct
    return pl.pallas_call(
        expert_kernel,
        grid_spec=pltpu.PrefetchScalarGridSpec(
            num_scalar_prefetch=1,
            grid=(local,),
            in_specs=[
                whole((length, width)),
                whole((length, width)),
                whole(c_pair[0].shape),
                whole(c_pair[1].shape),
                whole((experts, width)),
                pl.BlockSpec((pieces, 1, 3, part, width), lambda e, s: (0, e, 0, 0, 0)),
            ],
            out_specs=[per((slots, width))] * 2
            + [per((slots, units))] * 3
            + [whole((length, width))] * 4
            + [whole((experts, width))],
            scratch_shapes=[
                pltpu.VMEM((2, local * capacity, length), BF16),
                pltpu.VMEM((local, slots, width), BF16),
                pltpu.VMEM((local, slots, width), BF16),
                pltpu.VMEM((2, local * capacity, width), BF16),
                pltpu.VMEM((2, local * capacity, width), BF16),
                pltpu.VMEM((2, experts, length), F32),
                pltpu.VMEM((2, local, 1, length), F32),
            ],
        ),
        out_shape=[shape((local, slots, width), BF16)] * 2
        + [shape((local, slots, units), BF16)] * 3
        + [shape((length, width), BF16)] * 4
        + [shape((experts, width), F32)],
        compiler_params=pltpu.CompilerParams(vmem_limit_bytes=VMEM_LIMIT),
        cost_estimate=cost(5e9 * 6 * slots * local / 768),
        name="expert_chunk",
    )(first.reshape(1), *x_pair, *c_pair, router, weights)


def expert_weights_kernel(*refs):
    *inputs, out = refs
    n = len(inputs) // 5
    x, c, h, g, u = (inputs[i * n : (i + 1) * n] for i in range(5))
    for i, (left, right) in enumerate(((g, x), (u, x), (h, c))):

        @pl.when(pl.program_id(1) == i)
        def _():
            rows = [jnp.concatenate([a[0] for a in side], axis=0) for side in (left, right)]
            total = dot(*rows, TN)
            out[:, 0, 0] = total.astype(BF16).reshape(out.shape[0], out.shape[3], out.shape[4])


def expert_weight_grads(chunks, pieces):
    arrays = [a[i] for i in range(5) for a in chunks]
    local, _, width = chunks[0][0].shape
    units = chunks[0][2].shape[2]
    part = units // pieces
    slots = sum(a[0].shape[1] for a in chunks)
    return pl.pallas_call(
        expert_weights_kernel,
        grid=(local, 3),
        in_specs=[pl.BlockSpec((1,) + a.shape[1:], lambda e, i: (e, 0, 0)) for a in arrays],
        out_specs=pl.BlockSpec((pieces, 1, 1, part, width), lambda e, i: (0, e, i, 0, 0)),
        out_shape=jax.ShapeDtypeStruct((pieces, local, 3, part, width), BF16),
        compiler_params=pltpu.CompilerParams(vmem_limit_bytes=VMEM_LIMIT),
        cost_estimate=cost(2 * 6 * local * slots * units * width),
        name="expert_weights",
    )(*arrays)


def split_matmul(values, matrix, dims):
    high = values.astype(BF16)
    low = (values - high.astype(F32)).astype(BF16)
    return dot(high, matrix, dims) + dot(low, matrix, dims)


def exact_matmul(values, matrix, dims):
    return lax.dot_general(
        values, matrix.astype(F32), (dims, ((), ())),
        precision=lax.Precision.HIGHEST, preferred_element_type=F32,
    )


def shards(
    tokens,
    out_cotangent,
    assignment,
    norm_gains,
    attention_weights,
    router_weights,
    shared_weights,
    expert_weights,
):
    length, width = tokens.shape
    rows = attention_weights.shape[0]
    ranks = lax.axis_size("dp")
    local = expert_weights.shape[0]
    experts = local * ranks
    capacity = length * 6 // experts
    units = shared_weights.shape[2]

    n, k = positions(), cube_size()
    half = width // 2
    halves = (slice(0, half), slice(half, width))

    small = jnp.concatenate([norm_gains, router_weights], axis=1)
    small = jnp.pad(small, ((0, 0), (0, LANES - small.shape[1])))
    packed_in = jnp.concatenate([attention_weights[:, :3].reshape(rows, 3 * width), small], axis=1)
    packed_out = attention_weights[:, 3]
    turned = jnp.transpose(expert_weights, (0, 1, 3, 2))
    slots_in = line_fetch(packed_in)

    hot = jnp.sum(
        (assignment[:, :, None] == jnp.arange(experts)[None, None, :]).astype(F32), axis=1
    )
    before = (jnp.arange(length)[:, None] < jnp.arange(length)[None, :]).astype(BF16)
    earlier = dot(hot.astype(BF16), before, TN)
    places = jnp.where(hot.T > 0, jnp.minimum(earlier, float(capacity)), -1.0).astype(BF16)
    places = jnp.pad(places, ((0, 0), (0, width - length)))
    sent = jnp.concatenate([out_cotangent, places], axis=0)

    owner = block_order()
    true_row = (owner[:, None] * rows + jnp.arange(rows)[None, :]).reshape(width)
    order = (jnp.arange(width)[:, None] == true_row[None, :]).astype(BF16)
    tokens_float = tokens.astype(F32)
    tokens_rel = dot(tokens, order, NN).astype(BF16)
    c_rel = dot(out_cotangent, order, NN).astype(BF16)
    root_one = lax.rsqrt(jnp.mean(tokens_float * tokens_float, axis=-1, keepdims=True) + EPSILON)
    position = jnp.arange(length).astype(F32)
    frequency = 10000.0 ** (-jnp.arange(HEAD_SIZE // 2).astype(F32) * (2.0 / HEAD_SIZE))
    angle = position[:, None] * frequency[None, :]
    cosine = jnp.concatenate([jnp.cos(angle), jnp.cos(angle)], axis=1)
    sine = jnp.concatenate([-jnp.sin(angle), jnp.sin(angle)], axis=1)
    done = [slots_in, sent, order, tokens_rel, c_rel, root_one, cosine, sine]

    gather_in = DenseGather(after(slots_in, *done))
    line_out = LineGather(packed_out)
    for j in range(k):
        if j > 0:
            gather_in.join()
        got = gather_in.exchange(*done)
        swapped = [gather_in.swap_held(*done)] if j == k - 1 else []
        going = []
        while len(line_out.right) < n and (j == k - 1 or len(line_out.right) < 2):
            going = line_out.step(*(done if len(line_out.right) < 3 else []))
        done = [got, swapped, going]
    swapped = gather_in.swap_got(*done)
    slots_out = [line_out.slot(r) for r in range(n)]
    gather_out = DenseGather(slots_out)
    gather_out.exchange(*done)
    cots = LineGather(sent)
    going = cots.step(*done)
    project = gather_in.columns(0, 3 * width)
    small_full = gather_in.columns(3 * width, 3 * width + LANES)

    small_true = dot(order, small_full, NN)
    gain_one = small_full[:, 0].astype(F32)
    gain_two = small_true[:, 1]
    router = small_true[:, 2 : 2 + experts].T.astype(BF16)
    unit_one = tokens_rel.astype(F32) * root_one
    normed_one = (unit_one * gain_one).astype(BF16)
    routed = lax.all_gather(after(turned, *done), "fsdp", axis=0)
    projected = dot(normed_one, project, NN)
    done = [swapped, gather_out.got, projected]
    projected = after(projected, *done)
    for j in range(1, k):
        gather_out.join()
        projected = after(projected, *gather_out.held)
        gather_out.exchange(*done)
        done = [gather_out.got]
    query, key, value, mixed, lse = attention_forward(projected, cosine, sine)
    done = [gather_out.got, mixed, going]

    swapped = gather_out.swap_all(*done)
    if len(cots.right) < n:
        cots.step(*done)
    mixed_rel = dot(after(mixed, *done), order, NN).astype(BF16)
    out_full = gather_out.columns(0, width)
    hidden_res = tokens_float + dot(mixed_rel, out_full, NN)
    root_two = lax.rsqrt(jnp.mean(hidden_res * hidden_res, axis=-1, keepdims=True) + EPSILON)
    unit_two = hidden_res * root_two
    normed_two = (unit_two * gain_two).astype(BF16)
    shared_full = lax.all_gather(
        after(shared_weights.reshape(rows, 3 * units), normed_two), ("dp", "fsdp"), axis=0, tiled=True
    )
    done = [normed_two]

    rows_two = LineGather(normed_two)
    me = lax.axis_index("dp")
    chunks, x_pairs, c_pairs = [None] * n, [None] * n, [None] * n

    def pair_up(r, *others):
        x, c = after((rows_two.slot(r), cots.slot(r)), *others)
        x_pairs[r], c_pairs[r] = (x, core_swap(x)), (c, core_swap(c))
        return x_pairs[r], c_pairs[r]

    def chunk(r, *others):
        x, c = after((x_pairs[r], c_pairs[r]), *others)
        chunks[r] = expert_chunk((me * local).astype(jnp.int32), x, c, router, routed, capacity)
        return chunks[r]

    def shared_part(*others):
        rows_, c_ = after((normed_two, out_cotangent), *others)
        gate_up = dot(rows_, shared_full[:, : 2 * units], NN)
        active, slope = silu_parts(gate_up[:, :units])
        up = gate_up[:, units:]
        hidden = (active * up).astype(BF16)
        cot = dot(c_, shared_full[:, 2 * units :], NN)
        gate_up_cot = jnp.concatenate(
            [(cot * up * slope).astype(BF16), (cot * active).astype(BF16)], axis=1
        )
        rel = dot(rows_, order, NN).astype(BF16)
        grad = [
            jnp.concatenate(
                [dot(rel[:, cut], gate_up_cot, TN).astype(BF16),
                 dot(c_rel[:, cut], hidden, TN).astype(BF16)], axis=1,
            )
            for cut in halves
        ]
        out = dot(hidden, shared_full[:, 2 * units :], NT)
        return out, dot(gate_up_cot, shared_full[:, : 2 * units], NT), grad

    for at in range(n - 1):
        going = [rows_two.step(*done), cots.right[-1], cots.left[-1]]
        if at > 0 and len(cots.right) < n:
            going.append(cots.step(*done))
        beside = []
        if at == n - 4:
            beside.append(pair_up(0, *done))
        elif at == n - 3:
            beside.append(chunk(0, *done)[9])
        elif at == n - 2:
            pair_up(n // 2, *done)
            beside.append(chunk(n // 2, *done)[9])
        done = [going, beside]

    early = sorted({1, n - 1})
    late = [r for r in range(n) if r not in early and chunks[r] is None]
    back, back_slots = LineScatter(), [None] * n
    out_sums, out_slots = LineScatter(), [None] * n

    def own_part(r, *others):
        back_slots[r] = add_pair((chunks[r][5], core_swap(after(chunks[r][6], *others))))

    def out_part(r, *others):
        got = core_swap(after(chunks[r][8], *others))
        out_slots[r] = add_pair((chunks[r][7], got))
        return got

    done = [pair_up(early[0], *done)]
    for at, r in enumerate(early):
        moved = [pair_up(q, *done) for q in (early + late)[at + 1 :][:1]]
        done = [chunk(r, *done)[9], moved]
    for r in range(n):
        if chunks[r] is not None:
            own_part(r)

    results = {}
    for s in range(1, n):
        going = back.step(back_slots[n - s], back_slots[s], *done)
        held = back.sent
        made = []
        wanted = [r for r in late if r in (s + 1, n - s - 1)]
        for r in [r for r in range(n) if chunks[r] is not None and out_slots[r] is None][:2]:
            made.append(out_part(r, *held))
        for r in wanted:
            late.remove(r)
            pair_up(r, *held)
            made.append(chunk(r, *held)[9])
        if not late and not wanted:
            if "shared" not in results:
                results["shared"] = shared_part(*held)
                scatter = DenseScatter(*results["shared"][2])
                made.append(results["shared"])
            elif "experts" not in results:
                weights = expert_weight_grads(after(chunks, *held), lax.axis_size("fsdp"))
                results["experts"] = lax.psum_scatter(weights, "fsdp", scatter_dimension=0)
                made += [weights, scatter.swap(*held)]
            elif "exchange" not in results:
                results["exchange"] = scatter.exchange(0, *held)
                made.append(results["exchange"])
        done = [going, made]
        for r in wanted:
            own_part(r, *done)
    for r in range(n):
        if out_slots[r] is None:
            out_part(r, *done)
    shared_out, shared_back, _ = results["shared"]
    expert_sum = results["experts"]
    back_sum = back.total(back_slots[0])
    router_part = sum(a[9] for a in chunks)

    going_out = out_sums.step(out_slots[n - 1], out_slots[1], *done) if n > 1 else []
    moved = [scatter.exchange(i, *done) for i in range(1, k)]
    cotangent = out_cotangent.astype(F32)
    normed_two_cot = back_sum + shared_back
    scaled = normed_two_cot * gain_two
    gain_two_grad = jnp.sum(normed_two_cot * unit_two, axis=0)
    hidden_cot = cotangent + root_two * (
        scaled - unit_two * jnp.mean(scaled * unit_two, axis=-1, keepdims=True)
    )
    attn_cot = hidden_cot.astype(BF16)
    mixed_cot = dot(dot(attn_cot, out_full, NT).astype(BF16), order, NT).astype(BF16)
    cot_parts = attention_backward(query, key, value, mixed_cot, lse, cosine, sine)
    done = [cot_parts, going_out, moved]

    cot_parts = after(cot_parts, *done)
    going_out = out_sums.step(out_slots[n - 2], out_slots[2], *done) if n > 2 else []
    projected_cot = jnp.concatenate(cot_parts, axis=1)
    in_grad = [dot(normed_one[:, cut], projected_cot, TN).astype(BF16) for cut in halves[::-1]]
    in_scatter = DenseScatter(in_grad[1], in_grad[0])
    swap_in = in_scatter.swap()
    out_grad = [dot(after(mixed_rel, *in_grad)[:, cut], attn_cot, TN).astype(BF16) for cut in halves]
    out_scatter = DenseScatter(*out_grad)
    swap_out = out_scatter.swap()
    normed_one_cot = dot(after(projected_cot, *in_grad), project, NT)
    scaled_one = normed_one_cot * gain_one
    gain_one_grad = jnp.sum(normed_one_cot * unit_one, axis=0)
    true_part = exact_matmul(
        jnp.concatenate([gain_two_grad[None, :], router_part], axis=0), order, NN
    )
    small_grad = jnp.concatenate([gain_one_grad[None, :], true_part], axis=0)
    small_grad = jnp.pad(small_grad, ((0, LANES - small_grad.shape[0]), (0, 0))).T
    small_scatter = DenseScatter(small_grad[:half], small_grad[half:], F32)
    swap_small = small_scatter.swap()
    moved = []
    done = [swap_in, swap_small, swap_out, scaled_one, going_out, moved]

    for i in range(k):
        going = [in_scatter.exchange(i, *done, extra=small_scatter if i == 0 else None)]
        if i == 0:
            token_part = after(root_one, *done) * (
                scaled_one - unit_one * jnp.mean(scaled_one * unit_one, axis=-1, keepdims=True)
            )
            token_gradient = hidden_cot + split_matmul(token_part, order, NT)
            going += [token_gradient]
            for s in range(3, n):
                going_out = out_sums.step(out_slots[n - s], out_slots[s], *done)
            going.append(going_out)
        elif i == 1:
            going += [scatter.line(*done), expert_sum]
        done = [going]
    last = [in_scatter.line(*done)]
    last += [out_scatter.exchange(i, *done) for i in range(k)]
    out_scatter.line()
    shared_gradient = scatter.total().reshape(rows, 3, units)
    in_total = in_scatter.total()
    in_gradient = in_total[:, : 3 * width].reshape(rows, 3, width)
    out_gradient = out_scatter.total()
    attention_gradient = jnp.concatenate([in_gradient, out_gradient[:, None, :]], axis=1)
    small_gradient = in_total[:, 3 * width :]
    out_sum = out_sums.total(out_slots[0])
    block_output = (hidden_res + shared_out + out_sum).astype(BF16)
    expert_gradient = jnp.transpose(expert_sum, (0, 1, 3, 2)).astype(F32)
    return (
        block_output,
        token_gradient,
        small_gradient[:, :2],
        attention_gradient,
        small_gradient[:, 2 : 2 + experts],
        shared_gradient,
        expert_gradient,
    )


def solution(mesh):
    both = ("dp", "fsdp")
    return jax.shard_map(
        shards,
        mesh=mesh,
        in_specs=(
            P(both, None),
            P(both, None),
            P(both, None),
            P(both, None),
            P(both, None, None),
            P(both, None),
            P(both, None, None),
            P("dp", None, None, "fsdp"),
        ),
        out_specs=(
            P(both, None),
            P(both, None),
            P(both, None),
            P(both, None, None),
            P(both, None),
            P(both, None, None),
            P("dp", None, None, "fsdp"),
        ),
        check_vma=False,
    )
```

```python
import jax
import jax.numpy as jnp
from jax import lax
from jax.experimental import pallas as pl
from jax.experimental.pallas import tpu as pltpu
from jax.sharding import PartitionSpec as P

HEAD_SIZE = 128
TOPK = 7
EPSILON = 1e-06
MASKED = -1e30
LANES = 128
F32 = jnp.float32
BF16 = jnp.bfloat16
VMEM_LIMIT = 58 * 1024 * 1024


def after(values, *others):
    return lax.optimization_barrier((values, others))[0]


def core_swap(x):
    return lax.ppermute(x, "dp", [(d, d ^ 1) for d in range(lax.axis_size("dp"))])


def fsdp_swap(x, bit):
    return lax.ppermute(x, "fsdp", [(f, f ^ bit) for f in range(lax.axis_size("fsdp"))])


def positions():
    return lax.axis_size("dp") // 2


def line_fetch(x):
    n = positions()
    pairs = lambda r: [
        (2 * ((p + r) % n) + c, 2 * p + c) for p in range(n) for c in range(2)
    ]
    return [x] + [lax.ppermute(x, "dp", pairs(r)) for r in range(1, n)]


def line_return(slots, kind=BF16):
    n = positions()
    pairs = lambda r: [
        (2 * p + c, 2 * ((p + r) % n) + c) for p in range(n) for c in range(2)
    ]
    return [slots[0]] + [lax.ppermute(slots[r].astype(kind), "dp", pairs(r)) for r in range(1, n)]


def add_all(parts):
    return sum(a.astype(F32) for a in parts)


def line_send(x, step, first, last):
    pairs = [(2 * p + c, 2 * (p + step) + c) for p in range(first, last + 1) for c in range(2)]
    return lax.ppermute(x, "dp", pairs)


class LineGather:
    def __init__(self, x):
        self.right, self.left = [x], [x]
        self.n = positions()

    def step(self, *others):
        s = len(self.right)
        a, b = after((self.right[-1], self.left[-1]), *others)
        self.right.append(line_send(a, 1, s - 1, self.n - 2))
        self.left.append(line_send(b, -1, 1, self.n - s))
        return self.right[-1], self.left[-1]

    def slot(self, r, *others):
        if r == 0:
            return after(self.right[0], *others)
        p = lax.axis_index("dp") // 2
        near, far = after((self.left[r], self.right[self.n - r]), *others)
        return jnp.where(p + r < self.n, near, far)


class LineScatter:
    def __init__(self):
        self.right = self.left = None
        self.s = 0
        self.n = positions()

    def step(self, to_right, to_left, *others):
        self.s += 1
        s = self.s
        a, b = after((to_right, to_left), *others)
        if self.right is not None:
            a, b = a.astype(F32) + self.right.astype(F32), b.astype(F32) + self.left.astype(F32)
        a, b = lax.optimization_barrier((a.astype(BF16), b.astype(BF16)))
        self.sent = a, b
        self.right = line_send(a, 1, 0, s - 1)
        self.left = line_send(b, -1, self.n - s, self.n - 1)
        return self.right, self.left

    def total(self, own):
        if self.right is None:
            return own.astype(F32)
        return own.astype(F32) + self.right.astype(F32) + self.left.astype(F32)


def cube_size():
    return max(lax.axis_size("fsdp").bit_length() - 1, 1)


def cube_bit(part, j):
    return 1 << ((part + j) % cube_size())


def cube_masks(part):
    masks = [0]
    for j in range(cube_size()):
        masks = masks + [m ^ cube_bit(part, j) for m in masks]
    return masks


def add_pair(pair):
    return pair[0].astype(F32) + pair[1].astype(F32)


def dense_parts(slots):
    k = cube_size()
    return [jnp.concatenate(slots[part::k], axis=0) for part in range(k)]


class DenseGather:
    def __init__(self, slots):
        self.held = dense_parts(slots)
        self.j = 0

    def exchange(self, *others):
        self.held = after(self.held, *others)
        self.got = [fsdp_swap(a, cube_bit(part, self.j)) for part, a in enumerate(self.held)]
        self.j += 1
        return self.got

    def join(self):
        self.held = [jnp.concatenate(pair, axis=0) for pair in zip(self.held, self.got)]

    def swap_held(self, *others):
        self.first = core_swap(after(jnp.concatenate(self.held, axis=0), *others))
        return self.first

    def swap_got(self, *others):
        self.second = core_swap(after(jnp.concatenate(self.got, axis=0), *others))
        return self.second

    def swap_all(self, *others):
        both = jnp.concatenate(self.held + self.got, axis=0)
        both = core_swap(after(both, *others))
        size = sum(a.shape[0] for a in self.held)
        self.first, self.second = both[:size], both[size:]
        return both

    def pieces(self):
        own, other, at = [], [], 0
        for a, b in zip(self.held, self.got):
            size = a.shape[0]
            own += [a, b]
            other += [self.first[at : at + size], self.second[at : at + size]]
            at += size
        return own + other

    def columns(self, start, stop):
        return jnp.concatenate([a[:, start:stop] for a in self.pieces()], axis=0)


def block_order():
    n = positions()
    d, f = lax.axis_index("dp"), lax.axis_index("fsdp")
    order = []
    for cx in range(2):
        for part in range(cube_size()):
            for m in cube_masks(part):
                for r in range(n)[part :: cube_size()]:
                    device = ((d // 2 + r) % n) * 2 + (d % 2 ^ cx)
                    order.append(device * lax.axis_size("fsdp") + (f ^ m))
    return jnp.stack(order)


class DenseScatter:
    def __init__(self, own, other, kind=BF16):
        self.own, self.other, self.kind = own, other, kind

    def swap(self, *others):
        other = after(self.other.astype(self.kind), *others)
        self.got = core_swap(other)
        return self.got

    def cut(self, extra):
        total = add_pair((self.own, self.got))
        if extra is not None:
            total = jnp.concatenate([total, add_pair((extra.own, extra.got))], axis=1)
        n, k = positions(), cube_size()
        rows = total.shape[0] // (n * 2**k)
        self.parts, at = [], 0
        for part in range(k):
            size = 2**k * len(range(n)[part::k]) * rows
            self.parts.append(total[at : at + size])
            at += size
        self.rows = rows

    def exchange(self, i, *others, extra=None):
        j = cube_size() - 1 - i
        if i > 0:
            self.parts = [add_pair(pair) for pair in self.pairs]
        else:
            self.cut(extra)
        halves = [x.shape[0] // 2 for x in self.parts]
        sent = after([x[h:].astype(self.kind) for x, h in zip(self.parts, halves)], *others)
        self.pairs = [
            (x[:h], fsdp_swap(y, cube_bit(part, j)))
            for part, (x, y, h) in enumerate(zip(self.parts, sent, halves))
        ]
        return [b for _, b in self.pairs]

    def line(self, *others):
        n, k = positions(), cube_size()
        slots = [None] * n
        for part, pair in enumerate(self.pairs):
            got = add_pair(pair)
            for i, r in enumerate(range(n)[part::k]):
                slots[r] = got[i * self.rows : (i + 1) * self.rows]
        sent = after([x.astype(self.kind) for x in slots[1:]], *others)
        self.arrived = line_return([slots[0]] + sent, self.kind)
        return self.arrived[1:]

    def total(self):
        return add_all(self.arrived)


def dot(a, b, dims):
    return lax.dot_general(a, b, (dims, ((), ())), preferred_element_type=F32)


NN = ((1,), (0,))
NT = ((1,), (1,))
TN = ((0,), (0,))


def turn(x, cosine, sine):
    return x * cosine + pltpu.roll(x, HEAD_SIZE // 2, 1) * sine


def causal_scores(q, k):
    scores = dot(k, q, NT) * (HEAD_SIZE ** (-0.5))
    key = lax.broadcasted_iota(jnp.int32, scores.shape, 0)
    query = lax.broadcasted_iota(jnp.int32, scores.shape, 1)
    return jnp.where(key <= query, scores, MASKED)


def cost(flops, transcendentals=0):
    return pl.CostEstimate(
        flops=int(flops), transcendentals=int(transcendentals), bytes_accessed=int(flops // 400)
    )


def attention_forward_kernel(qp, kp, vp, cosine, sine, q_out, k_out, v_out, mixed_out, lse_out):
    q = turn(qp[...], cosine[...], sine[...]).astype(BF16)
    k = turn(kp[...], cosine[...], sine[...]).astype(BF16)
    v = vp[...].astype(BF16)
    q_out[...] = q
    k_out[...] = k
    v_out[...] = v
    scores = causal_scores(q, k)
    peak = jnp.max(scores, axis=0, keepdims=True)
    expo = jnp.exp(scores - peak)
    totals = jnp.sum(expo, axis=0, keepdims=True)
    lse_out[0] = peak + jnp.log(totals)
    probability = (expo * (1.0 / totals)).astype(BF16)
    mixed_out[...] = dot(probability, v, TN).astype(BF16)


def attention_forward(projected, cosine, sine):
    length = projected.shape[0]
    width = projected.shape[1] // 3
    heads = width // HEAD_SIZE
    block = (length, HEAD_SIZE)
    table = pl.BlockSpec(block, lambda h: (0, 0))
    column = pl.BlockSpec(block, lambda h: (0, h))
    rows = jax.ShapeDtypeStruct((length, width), BF16)
    return pl.pallas_call(
        attention_forward_kernel,
        grid=(heads,),
        in_specs=[
            column,
            pl.BlockSpec(block, lambda h: (0, heads + h)),
            pl.BlockSpec(block, lambda h: (0, 2 * heads + h)),
            table,
            table,
        ],
        out_specs=[column] * 4 + [pl.BlockSpec((1, 1, length), lambda h: (h, 0, 0))],
        out_shape=[rows] * 4 + [jax.ShapeDtypeStruct((heads, 1, length), F32)],
        compiler_params=pltpu.CompilerParams(vmem_limit_bytes=VMEM_LIMIT),
        cost_estimate=cost(14e9),
        name="attention_forward",
    )(projected, projected, projected, cosine, sine)


def attention_backward_kernel(q_in, k_in, v_in, d_in, lse, cosine, sine, dq_out, dk_out, dv_out):
    q, k, v, d = q_in[...], k_in[...], v_in[...], d_in[...]
    scale = HEAD_SIZE ** (-0.5)
    probability = jnp.exp(causal_scores(q, k) - lse[0])
    dv_out[...] = dot(probability.astype(BF16), d, NN).astype(BF16)
    prob_cot = dot(v, d, NT)
    row_dot = jnp.sum(probability * prob_cot, axis=0, keepdims=True)
    score_cot = (probability * (prob_cot - row_dot)).astype(BF16)
    dk = dot(score_cot, q, NN) * scale
    dq = dot(score_cot, k, TN) * scale
    dq_out[...] = turn(dq, cosine[...], -sine[...]).astype(BF16)
    dk_out[...] = turn(dk, cosine[...], -sine[...]).astype(BF16)


def attention_backward(q, k, v, mixed_cot, lse, cosine, sine):
    length, width = q.shape
    heads = width // HEAD_SIZE
    block = (length, HEAD_SIZE)
    table = pl.BlockSpec(block, lambda h: (0, 0))
    column = pl.BlockSpec(block, lambda h: (0, h))
    return pl.pallas_call(
        attention_backward_kernel,
        grid=(heads,),
        in_specs=[column] * 4
        + [pl.BlockSpec((1, 1, length), lambda h: (h, 0, 0)), table, table],
        out_specs=[column] * 3,
        out_shape=[jax.ShapeDtypeStruct((length, width), BF16)] * 3,
        compiler_params=pltpu.CompilerParams(vmem_limit_bytes=VMEM_LIMIT),
        cost_estimate=cost(15e9),
        name="attention_backward",
    )(q, k, v, mixed_cot, lse, cosine, sine)


def silu_parts(gate_value):
    sigmoid_value = jax.nn.sigmoid(gate_value)
    return (gate_value * sigmoid_value, sigmoid_value * (1.0 + gate_value * (1.0 - sigmoid_value)))


def expert_kernel(
    first, x_own, x_other, c_own, c_other, router, weights,
    x_out, c_out, h_out, g_out, u_out, cot_own, cot_other, out_own, out_other, router_out,
    picks, xs, cs, x_cots, ys, shares, backs,
):
    length, width = x_own.shape
    capacity = x_out.shape[1] // 2
    experts = router.shape[0]
    local = pl.num_programs(0)
    count = picks.shape[1] // capacity
    step = pl.program_id(0)
    sources = ((x_own, c_own), (x_other, c_other))
    w_gate, w_up, w_down = (weights[:, 0, i].reshape(-1, width) for i in range(3))
    expert_row = lax.broadcasted_iota(jnp.int32, (experts, length), 0)
    slot_row = lax.broadcasted_iota(jnp.int32, (capacity, length), 0).astype(F32)

    def row_of(table, index):
        return jnp.sum(jnp.where(expert_row == index, table, 0.0), axis=0, keepdims=True)

    @pl.when(step == 0)
    def _():
        for at, (x_ref, c_ref) in enumerate(sources):
            ranks = c_ref[length : length + experts, :length].astype(F32)
            logits = dot(router[...], x_ref[...], NT)
            expo = jnp.exp(logits - jnp.max(logits, axis=0, keepdims=True))
            shares[at] = expo * (1.0 / jnp.sum(expo, axis=0, keepdims=True))
            pick = jnp.concatenate(
                [jnp.where(slot_row == row_of(ranks, first[0] + e), 1.0, 0.0) for e in range(count)],
                axis=0,
            ).astype(BF16)
            picks[at] = pick
            x = dot(pick, x_ref[...], NN).astype(BF16)
            c = dot(pick, c_ref[:length, :], NN).astype(BF16)
            for e in range(count):
                low, high = e * capacity, (e + 1) * capacity
                xs[e, at * capacity : (at + 1) * capacity, :] = x[low:high]
                cs[e, at * capacity : (at + 1) * capacity, :] = c[low:high]

    x = xs[step]
    c = cs[step]
    gate_columns = []
    for at, (_, c_ref) in enumerate(sources):
        ranks = c_ref[length : length + experts, :length].astype(F32)
        chosen = jnp.where(ranks >= 0.0, shares[at], 0.0)
        gate = row_of(chosen, first[0] + step) / jnp.sum(chosen, axis=0, keepdims=True)
        pick = picks[at, pl.ds(pl.multiple_of(step * capacity, 32), capacity), :].astype(F32)
        gate_columns.append(jnp.sum(pick * gate, axis=1, keepdims=True))
    gates = jnp.concatenate(gate_columns, axis=0)
    x_out[0] = x
    c_out[0] = (gates * c.astype(F32)).astype(BF16)
    gate_value = dot(x, w_gate, NT)
    up_value = dot(x, w_up, NT)
    raw_cot = dot(c, w_down, NT)
    active, slope = silu_parts(gate_value)
    hidden16 = (active * up_value).astype(BF16)
    hidden = hidden16.astype(F32)
    gate_cot = jnp.sum(raw_cot * hidden, axis=1, keepdims=True)
    hidden_cot = gates * raw_cot
    h_out[0] = hidden16
    g16 = (hidden_cot * up_value * slope).astype(BF16)
    u16 = (hidden_cot * active).astype(BF16)
    g_out[0] = g16
    u_out[0] = u16
    x_cot = (dot(g16, w_gate, NN) + dot(u16, w_up, NN)).astype(BF16)
    y = dot((gates * hidden).astype(BF16), w_down, NN).astype(BF16)
    for at in range(2):
        low, high = at * capacity, (at + 1) * capacity
        rows = pl.ds(pl.multiple_of(step * capacity, 32), capacity)
        x_cots[at, rows, :] = x_cot[low:high]
        ys[at, rows, :] = y[low:high]
        pick = picks[at, rows, :].astype(F32)
        backs[at, step] = jnp.sum(pick * gate_cot[low:high], axis=0, keepdims=True)

    @pl.when(step == local - 1)
    def _():
        for at, (x_ref, c_ref) in enumerate(sources):
            ranks = c_ref[length : length + experts, :length].astype(F32)
            probability = shares[at]
            chosen = jnp.where(ranks >= 0.0, probability, 0.0)
            total = jnp.sum(chosen, axis=0, keepdims=True)
            direct = jnp.zeros_like(chosen)
            shift = jnp.zeros_like(total)
            for e in range(count):
                back = backs[at, e]
                shift += back * row_of(chosen, first[0] + e)
                direct += jnp.where(expert_row == first[0] + e, back / total, 0.0)
            prob_cot = jnp.where(ranks >= 0.0, direct - shift / (total * total), 0.0)
            inner = jnp.sum(prob_cot * probability, axis=0, keepdims=True)
            logit_cot = (probability * (prob_cot - inner)).astype(BF16)
            cot = dot(picks[at], x_cots[at], TN) + dot(logit_cot, router[...], TN)
            out = dot(picks[at], ys[at], TN)
            (cot_own, cot_other)[at][...] = cot.astype(BF16)
            (out_own, out_other)[at][...] = out.astype(BF16)
            part = dot(logit_cot, x_ref[...], NN)
            router_out[...] = part if at == 0 else router_out[...] + part


def expert_chunk(first, x_pair, c_pair, router, weights, capacity):
    length, width = x_pair[0].shape
    pieces, local, _, part, _ = weights.shape
    units = pieces * part
    experts = router.shape[0]
    whole = lambda shape: pl.BlockSpec(
        shape, lambda e, s: (0,) * len(shape), pipeline_mode=pl.Buffered(1)
    )
    per = lambda shape: pl.BlockSpec((1,) + shape, lambda e, s: (e,) + (0,) * len(shape))
    slots = 2 * capacity
    shape = jax.ShapeDtypeStruct
    return pl.pallas_call(
        expert_kernel,
        grid_spec=pltpu.PrefetchScalarGridSpec(
            num_scalar_prefetch=1,
            grid=(local,),
            in_specs=[
                whole((length, width)),
                whole((length, width)),
                whole(c_pair[0].shape),
                whole(c_pair[1].shape),
                whole((experts, width)),
                pl.BlockSpec((pieces, 1, 3, part, width), lambda e, s: (0, e, 0, 0, 0)),
            ],
            out_specs=[per((slots, width))] * 2
            + [per((slots, units))] * 3
            + [whole((length, width))] * 4
            + [whole((experts, width))],
            scratch_shapes=[
                pltpu.VMEM((2, local * capacity, length), BF16),
                pltpu.VMEM((local, slots, width), BF16),
                pltpu.VMEM((local, slots, width), BF16),
                pltpu.VMEM((2, local * capacity, width), BF16),
                pltpu.VMEM((2, local * capacity, width), BF16),
                pltpu.VMEM((2, experts, length), F32),
                pltpu.VMEM((2, local, 1, length), F32),
            ],
        ),
        out_shape=[shape((local, slots, width), BF16)] * 2
        + [shape((local, slots, units), BF16)] * 3
        + [shape((length, width), BF16)] * 4
        + [shape((experts, width), F32)],
        compiler_params=pltpu.CompilerParams(vmem_limit_bytes=VMEM_LIMIT),
        cost_estimate=cost(5e9 * 6 * slots * local / 768),
        name="expert_chunk",
    )(first.reshape(1), *x_pair, *c_pair, router, weights)


def expert_weights_kernel(*refs):
    *inputs, out = refs
    n = len(inputs) // 5
    x, c, h, g, u = (inputs[i * n : (i + 1) * n] for i in range(5))
    for i, (left, right) in enumerate(((g, x), (u, x), (h, c))):

        @pl.when(pl.program_id(1) == i)
        def _():
            rows = [jnp.concatenate([a[0] for a in side], axis=0) for side in (left, right)]
            total = dot(*rows, TN)
            out[:, 0, 0] = total.astype(BF16).reshape(out.shape[0], out.shape[3], out.shape[4])


def expert_weight_grads(chunks, pieces):
    arrays = [a[i] for i in range(5) for a in chunks]
    local, _, width = chunks[0][0].shape
    units = chunks[0][2].shape[2]
    part = units // pieces
    slots = sum(a[0].shape[1] for a in chunks)
    return pl.pallas_call(
        expert_weights_kernel,
        grid=(local, 3),
        in_specs=[pl.BlockSpec((1,) + a.shape[1:], lambda e, i: (e, 0, 0)) for a in arrays],
        out_specs=pl.BlockSpec((pieces, 1, 1, part, width), lambda e, i: (0, e, i, 0, 0)),
        out_shape=jax.ShapeDtypeStruct((pieces, local, 3, part, width), BF16),
        compiler_params=pltpu.CompilerParams(vmem_limit_bytes=VMEM_LIMIT),
        cost_estimate=cost(2 * 6 * local * slots * units * width),
        name="expert_weights",
    )(*arrays)


def shared_kernel(x, c, c_rel, weights, order, out, back, own, other):
    width, columns = weights.shape
    units = columns // 3
    half = width // 2
    gate_value = dot(x[...], weights[:, :units], NN)
    up = dot(x[...], weights[:, units : 2 * units], NN)
    active, slope = silu_parts(gate_value)
    hidden = (active * up).astype(BF16)
    cot = dot(c[...], weights[:, 2 * units :], NN)
    gate_cot = (cot * up * slope).astype(BF16)
    up_cot = (cot * active).astype(BF16)
    out[...] = dot(hidden, weights[:, 2 * units :], NT)
    back[...] = dot(gate_cot, weights[:, :units], NT) + dot(
        up_cot, weights[:, units : 2 * units], NT
    )
    rel = dot(x[...], order[...], NN).astype(BF16)
    for cut, grad in ((slice(0, half), own), (slice(half, width), other)):
        grad[:, :units] = dot(rel[:, cut], gate_cot, TN).astype(BF16)
        grad[:, units : 2 * units] = dot(rel[:, cut], up_cot, TN).astype(BF16)
        grad[:, 2 * units :] = dot(c_rel[:, cut], hidden, TN).astype(BF16)


def shared_expert(x, c, c_rel, weights, order):
    width, columns = weights.shape
    shape = jax.ShapeDtypeStruct
    return pl.pallas_call(
        shared_kernel,
        out_shape=[shape(x.shape, F32)] * 2 + [shape((width // 2, columns), BF16)] * 2,
        compiler_params=pltpu.CompilerParams(vmem_limit_bytes=VMEM_LIMIT),
        cost_estimate=cost(30e9),
        name="shared_expert",
    )(x, c, c_rel, weights, order)


def split_matmul(values, matrix, dims):
    high = values.astype(BF16)
    low = (values - high.astype(F32)).astype(BF16)
    return dot(high, matrix, dims) + dot(low, matrix, dims)


def exact_matmul(values, matrix, dims):
    return lax.dot_general(
        values, matrix.astype(F32), (dims, ((), ())),
        precision=lax.Precision.HIGHEST, preferred_element_type=F32,
    )


def shards(
    tokens,
    out_cotangent,
    assignment,
    norm_gains,
    attention_weights,
    router_weights,
    shared_weights,
    expert_weights,
):
    length, width = tokens.shape
    rows = attention_weights.shape[0]
    ranks = lax.axis_size("dp")
    local = expert_weights.shape[0]
    experts = local * ranks
    capacity = length * 6 // experts
    units = shared_weights.shape[2]

    n, k = positions(), cube_size()
    half = width // 2
    halves = (slice(0, half), slice(half, width))

    small = jnp.concatenate([norm_gains, router_weights], axis=1)
    small = jnp.pad(small, ((0, 0), (0, LANES - small.shape[1])))
    packed_in = jnp.concatenate([attention_weights[:, :3].reshape(rows, 3 * width), small], axis=1)
    packed_out = attention_weights[:, 3]
    turned = jnp.transpose(expert_weights, (0, 1, 3, 2))
    slots_in = line_fetch(packed_in)

    hot = jnp.sum(
        (assignment[:, :, None] == jnp.arange(experts)[None, None, :]).astype(F32), axis=1
    )
    before = (jnp.arange(length)[:, None] < jnp.arange(length)[None, :]).astype(BF16)
    earlier = dot(hot.astype(BF16), before, TN)
    places = jnp.where(hot.T > 0, jnp.minimum(earlier, float(capacity)), -1.0).astype(BF16)
    places = jnp.pad(places, ((0, 0), (0, width - length)))
    sent = jnp.concatenate([out_cotangent, places], axis=0)

    owner = block_order()
    true_row = (owner[:, None] * rows + jnp.arange(rows)[None, :]).reshape(width)
    order = (jnp.arange(width)[:, None] == true_row[None, :]).astype(BF16)
    tokens_float = tokens.astype(F32)
    tokens_rel = dot(tokens, order, NN).astype(BF16)
    c_rel = dot(out_cotangent, order, NN).astype(BF16)
    root_one = lax.rsqrt(jnp.mean(tokens_float * tokens_float, axis=-1, keepdims=True) + EPSILON)
    position = jnp.arange(length).astype(F32)
    frequency = 10000.0 ** (-jnp.arange(HEAD_SIZE // 2).astype(F32) * (2.0 / HEAD_SIZE))
    angle = position[:, None] * frequency[None, :]
    cosine = jnp.concatenate([jnp.cos(angle), jnp.cos(angle)], axis=1)
    sine = jnp.concatenate([-jnp.sin(angle), jnp.sin(angle)], axis=1)
    done = [slots_in, sent, order, tokens_rel, c_rel, root_one, cosine, sine]

    gather_in = DenseGather(after(slots_in, *done))
    line_out = LineGather(packed_out)
    for j in range(k):
        if j > 0:
            gather_in.join()
        got = gather_in.exchange(*done)
        swapped = [gather_in.swap_held(*done)] if j == k - 1 else []
        going = []
        while len(line_out.right) < n and (j == k - 1 or len(line_out.right) < 2):
            going = line_out.step(*(done if len(line_out.right) < 3 else []))
        done = [got, swapped, going]
    swapped = gather_in.swap_got(*done)
    slots_out = [line_out.slot(r) for r in range(n)]
    gather_out = DenseGather(slots_out)
    gather_out.exchange(*done)
    cots = LineGather(sent)
    going = cots.step(*done)
    packed_full = jnp.concatenate(gather_in.pieces(), axis=0)
    project, small_full = packed_full[:, : 3 * width], packed_full[:, 3 * width :]

    small_true = dot(order, small_full, NN)
    gain_one = small_full[:, 0].astype(F32)
    gain_two = small_true[:, 1]
    router = small_true[:, 2 : 2 + experts].T.astype(BF16)
    unit_one = tokens_rel.astype(F32) * root_one
    normed_one = (unit_one * gain_one).astype(BF16)
    routed = lax.all_gather(after(turned, *done), "fsdp", axis=0)
    projected = dot(normed_one, project, NN)
    done = [swapped, gather_out.got, projected]
    projected = after(projected, *done)
    for j in range(1, k):
        gather_out.join()
        projected = after(projected, *gather_out.held)
        gather_out.exchange(*done)
        done = [gather_out.got]
    query, key, value, mixed, lse = attention_forward(projected, cosine, sine)
    done = [gather_out.got, mixed, going]

    swapped = gather_out.swap_all(*done)
    if len(cots.right) < n:
        cots.step(*done)
    mixed_rel = dot(after(mixed, *done), order, NN).astype(BF16)
    out_full = gather_out.columns(0, width)
    hidden_res = tokens_float + dot(mixed_rel, out_full, NN)
    root_two = lax.rsqrt(jnp.mean(hidden_res * hidden_res, axis=-1, keepdims=True) + EPSILON)
    unit_two = hidden_res * root_two
    normed_two = (unit_two * gain_two).astype(BF16)
    done = [normed_two]

    rows_two = LineGather(normed_two)
    me = lax.axis_index("dp")
    chunks, x_pairs, c_pairs = [None] * n, [None] * n, [None] * n

    def pair_up(r, *others):
        x, c = rows_two.slot(r, *others), cots.slot(r, *others)
        x_pairs[r], c_pairs[r] = (x, core_swap(x)), (c, core_swap(c))
        return x_pairs[r], c_pairs[r]

    def chunk(r, *others):
        x, c = after((x_pairs[r], c_pairs[r]), *others)
        chunks[r] = expert_chunk((me * local).astype(jnp.int32), x, c, router, routed, capacity)
        return chunks[r]

    def shared_part(*others):
        rows_ = after(normed_two, *others)
        out, back, *grad = shared_expert(rows_, out_cotangent, c_rel, shared_full, order)
        return out, back, grad

    for at in range(n - 1):
        if at == n - 2:
            done = [pair_up(n // 2, *done)]
        going = [rows_two.step(*done), cots.right[-1], cots.left[-1]]
        if at > 0 and len(cots.right) < n:
            going.append(cots.step(*done))
        beside = []
        if at == n - 4:
            beside.append(pair_up(0, *done))
        elif at == n - 3:
            beside.append(chunk(0, *done)[9])
        elif at == n - 2:
            beside.append(chunk(n // 2, *done)[9])
        done = [going, beside]

    early = sorted({1, n - 1})
    late = [r for r in range(n) if r not in early and chunks[r] is None]
    back, back_slots = LineScatter(), [None] * n
    out_sums, out_slots = LineScatter(), [None] * n

    def own_part(r, *others):
        back_slots[r] = add_pair((chunks[r][5], core_swap(after(chunks[r][6], *others))))

    def out_part(r, *others):
        got = core_swap(after(chunks[r][8], *others))
        out_slots[r] = add_pair((chunks[r][7], got))
        return got

    shared_full = lax.all_gather(
        after(shared_weights.reshape(rows, 3 * units), *done), ("dp", "fsdp"), axis=0, tiled=True
    )
    done = [pair_up(early[0], *done)]
    for at, r in enumerate(early):
        moved = [pair_up(q, *done) for q in (early + late)[at + 1 :][:1]]
        done = [chunk(r, *done)[9], moved]
    for r in range(n):
        if chunks[r] is not None:
            own_part(r)

    results = {}
    for s in range(1, n):
        going = back.step(back_slots[n - s], back_slots[s], *done)
        held = back.sent
        made = []
        wanted = [r for r in late if r in (s + 1, n - s - 1)] or ([0] if late == [0] else [])
        for r in [r for r in range(n) if chunks[r] is not None and out_slots[r] is None][:2]:
            made.append(out_part(r, *held))
        for r in wanted:
            late.remove(r)
            if x_pairs[r] is None:
                pair_up(r, *held)
            made.append(chunk(r, *held)[9])
        if not late and not wanted:
            if "shared" not in results:
                results["shared"] = shared_part(*held)
                made.append(results["shared"])
            elif "experts" not in results:
                weights = expert_weight_grads(after(chunks, *held), lax.axis_size("fsdp"))
                scatter = DenseScatter(*results["shared"][2])
                results["experts"] = weights
                made += [weights, scatter.swap(*held)]
            elif "exchange" not in results:
                results["experts"] = lax.psum_scatter(
                    after(results["experts"], *done), "fsdp", scatter_dimension=0
                )
                results["exchange"] = scatter.exchange(0, *done)
                made.append(results["exchange"])
        done = [going, made]
        for r in wanted:
            own_part(r, *done)
    for r in range(n):
        if out_slots[r] is None:
            out_part(r, *done)
    expert_sum = results["experts"]
    shared_out, shared_back, _ = results["shared"]
    back_sum = back.total(back_slots[0])
    router_part = sum(a[9] for a in chunks)

    going_out = out_sums.step(out_slots[n - 1], out_slots[1], *done) if n > 1 else []
    cotangent = out_cotangent.astype(F32)
    normed_two_cot = back_sum + shared_back
    scaled = normed_two_cot * gain_two
    gain_two_grad = jnp.sum(normed_two_cot * unit_two, axis=0)
    hidden_cot = cotangent + root_two * (
        scaled - unit_two * jnp.mean(scaled * unit_two, axis=-1, keepdims=True)
    )
    attn_cot = hidden_cot.astype(BF16)
    moved = [scatter.exchange(i, *done) for i in range(1, k)]
    mixed_cot = dot(dot(attn_cot, out_full, NT).astype(BF16), order, NT).astype(BF16)
    cot_parts = attention_backward(query, key, value, mixed_cot, lse, cosine, sine)
    done = [cot_parts, going_out, moved]

    cot_parts = after(cot_parts, *done)
    going_out = out_sums.step(out_slots[n - 2], out_slots[2], *done) if n > 2 else []
    projected_cot = jnp.concatenate(cot_parts, axis=1)
    in_grad = [dot(normed_one[:, cut], projected_cot, TN).astype(BF16) for cut in halves[::-1]]
    in_scatter = DenseScatter(in_grad[1], in_grad[0])
    swap_in = in_scatter.swap()
    out_grad = [dot(after(mixed_rel, *in_grad)[:, cut], attn_cot, TN).astype(BF16) for cut in halves]
    out_scatter = DenseScatter(*out_grad)
    swap_out = out_scatter.swap()
    normed_one_cot = dot(after(projected_cot, *in_grad), project, NT)
    scaled_one = normed_one_cot * gain_one
    gain_one_grad = jnp.sum(normed_one_cot * unit_one, axis=0)
    true_part = exact_matmul(
        jnp.concatenate([gain_two_grad[None, :], router_part], axis=0), order, NN
    )
    small_grad = jnp.concatenate([gain_one_grad[None, :], true_part], axis=0)
    small_grad = jnp.pad(small_grad, ((0, LANES - small_grad.shape[0]), (0, 0))).T
    small_scatter = DenseScatter(small_grad[:half], small_grad[half:], F32)
    swap_small = small_scatter.swap()
    moved = []
    done = [swap_in, swap_small, swap_out, scaled_one, going_out, moved]

    for i in range(k):
        going = [in_scatter.exchange(i, *done, extra=small_scatter if i == 0 else None)]
        if i == 0:
            token_part = after(root_one, *done) * (
                scaled_one - unit_one * jnp.mean(scaled_one * unit_one, axis=-1, keepdims=True)
            )
            token_gradient = hidden_cot + split_matmul(token_part, order, NT)
            going += [token_gradient]
            for s in range(3, n):
                going_out = out_sums.step(out_slots[n - s], out_slots[s], *done)
            going.append(going_out)
        elif i == 1:
            going += [scatter.line(*done), expert_sum]
        done = [going]
    last = [in_scatter.line(*done)]
    last += [out_scatter.exchange(i, *done) for i in range(k)]
    out_scatter.line()
    shared_gradient = scatter.total().reshape(rows, 3, units)
    in_total = in_scatter.total()
    in_gradient = in_total[:, : 3 * width].reshape(rows, 3, width)
    out_gradient = out_scatter.total()
    attention_gradient = jnp.concatenate([in_gradient, out_gradient[:, None, :]], axis=1)
    small_gradient = in_total[:, 3 * width :]
    out_sum = out_sums.total(out_slots[0])
    block_output = (hidden_res + shared_out + out_sum).astype(BF16)
    expert_gradient = jnp.transpose(expert_sum, (0, 1, 3, 2)).astype(F32)
    return (
        block_output,
        token_gradient,
        small_gradient[:, :2],
        attention_gradient,
        small_gradient[:, 2 : 2 + experts],
        shared_gradient,
        expert_gradient,
    )


def solution(mesh):
    both = ("dp", "fsdp")
    return jax.shard_map(
        shards,
        mesh=mesh,
        in_specs=(
            P(both, None),
            P(both, None),
            P(both, None),
            P(both, None),
            P(both, None, None),
            P(both, None),
            P(both, None, None),
            P("dp", None, None, "fsdp"),
        ),
        out_specs=(
            P(both, None),
            P(both, None),
            P(both, None),
            P(both, None, None),
            P(both, None),
            P(both, None, None),
            P("dp", None, None, "fsdp"),
        ),
        check_vma=False,
    )
```

```python
import jax
import jax.numpy as jnp
from jax import lax
from jax.experimental import pallas as pl
from jax.experimental.pallas import tpu as pltpu
from jax.sharding import PartitionSpec as P

HEAD_SIZE = 128
TOPK = 7
EPSILON = 1e-06
MASKED = -1e30
LANES = 128
F32 = jnp.float32
BF16 = jnp.bfloat16
VMEM_LIMIT = 58 * 1024 * 1024


def after(values, *others):
    return lax.optimization_barrier((values, others))[0]


def core_swap(x):
    return lax.ppermute(x, "dp", [(d, d ^ 1) for d in range(lax.axis_size("dp"))])


def fsdp_swap(x, bit):
    return lax.ppermute(x, "fsdp", [(f, f ^ bit) for f in range(lax.axis_size("fsdp"))])


def positions():
    return lax.axis_size("dp") // 2


def line_fetch(x):
    n = positions()
    pairs = lambda r: [
        (2 * ((p + r) % n) + c, 2 * p + c) for p in range(n) for c in range(2)
    ]
    return [x] + [lax.ppermute(x, "dp", pairs(r)) for r in range(1, n)]


def line_return(slots, kind=BF16):
    n = positions()
    pairs = lambda r: [
        (2 * p + c, 2 * ((p + r) % n) + c) for p in range(n) for c in range(2)
    ]
    return [slots[0]] + [lax.ppermute(slots[r].astype(kind), "dp", pairs(r)) for r in range(1, n)]


def add_all(parts):
    return sum(a.astype(F32) for a in parts)


def line_send(x, step, first, last):
    pairs = [(2 * p + c, 2 * (p + step) + c) for p in range(first, last + 1) for c in range(2)]
    return lax.ppermute(x, "dp", pairs)


class LineGather:
    def __init__(self, x):
        self.right, self.left = [x], [x]
        self.n = positions()

    def step(self, *others):
        s = len(self.right)
        a, b = after((self.right[-1], self.left[-1]), *others)
        self.right.append(line_send(a, 1, s - 1, self.n - 2))
        self.left.append(line_send(b, -1, 1, self.n - s))
        return self.right[-1], self.left[-1]

    def slot(self, r, *others):
        if r == 0:
            return after(self.right[0], *others)
        p = lax.axis_index("dp") // 2
        near, far = after((self.left[r], self.right[self.n - r]), *others)
        return jnp.where(p + r < self.n, near, far)


class LineScatter:
    def __init__(self):
        self.right = self.left = None
        self.s = 0
        self.n = positions()

    def step(self, to_right, to_left, *others):
        self.s += 1
        s = self.s
        a, b = after((to_right, to_left), *others)
        if self.right is not None:
            a, b = a.astype(F32) + self.right.astype(F32), b.astype(F32) + self.left.astype(F32)
        a, b = lax.optimization_barrier((a.astype(BF16), b.astype(BF16)))
        self.sent = a, b
        self.right = line_send(a, 1, 0, s - 1)
        self.left = line_send(b, -1, self.n - s, self.n - 1)
        return self.right, self.left

    def total(self, own):
        if self.right is None:
            return own.astype(F32)
        return own.astype(F32) + self.right.astype(F32) + self.left.astype(F32)


def cube_size():
    return max(lax.axis_size("fsdp").bit_length() - 1, 1)


def cube_bit(part, j):
    return 1 << ((part + j) % cube_size())


def cube_masks(part):
    masks = [0]
    for j in range(cube_size()):
        masks = masks + [m ^ cube_bit(part, j) for m in masks]
    return masks


def add_pair(pair):
    return pair[0].astype(F32) + pair[1].astype(F32)


def dense_parts(slots):
    k = cube_size()
    return [jnp.concatenate(slots[part::k], axis=0) for part in range(k)]


class DenseGather:
    def __init__(self, slots):
        self.held = dense_parts(slots)
        self.j = 0

    def exchange(self, *others):
        self.held = after(self.held, *others)
        self.got = [fsdp_swap(a, cube_bit(part, self.j)) for part, a in enumerate(self.held)]
        self.j += 1
        return self.got

    def join(self):
        self.held = [jnp.concatenate(pair, axis=0) for pair in zip(self.held, self.got)]

    def swap_held(self, *others):
        self.first = core_swap(after(jnp.concatenate(self.held, axis=0), *others))
        return self.first

    def swap_got(self, *others):
        self.second = core_swap(after(jnp.concatenate(self.got, axis=0), *others))
        return self.second

    def swap_all(self, *others):
        both = jnp.concatenate(self.held + self.got, axis=0)
        both = core_swap(after(both, *others))
        size = sum(a.shape[0] for a in self.held)
        self.first, self.second = both[:size], both[size:]
        return both

    def pieces(self):
        own, other, at = [], [], 0
        for a, b in zip(self.held, self.got):
            size = a.shape[0]
            own += [a, b]
            other += [self.first[at : at + size], self.second[at : at + size]]
            at += size
        return own + other

    def columns(self, start, stop):
        return jnp.concatenate([a[:, start:stop] for a in self.pieces()], axis=0)


def block_order():
    n = positions()
    d, f = lax.axis_index("dp"), lax.axis_index("fsdp")
    order = []
    for cx in range(2):
        for part in range(cube_size()):
            for m in cube_masks(part):
                for r in range(n)[part :: cube_size()]:
                    device = ((d // 2 + r) % n) * 2 + (d % 2 ^ cx)
                    order.append(device * lax.axis_size("fsdp") + (f ^ m))
    return jnp.stack(order)


class DenseScatter:
    def __init__(self, own, other, kind=BF16):
        self.own, self.other, self.kind = own, other, kind

    def swap(self, *others):
        other = after(self.other.astype(self.kind), *others)
        self.got = core_swap(other)
        return self.got

    def cut(self, extra):
        total = add_pair((self.own, self.got))
        if extra is not None:
            total = jnp.concatenate([total, add_pair((extra.own, extra.got))], axis=1)
        n, k = positions(), cube_size()
        rows = total.shape[0] // (n * 2**k)
        self.parts, at = [], 0
        for part in range(k):
            size = 2**k * len(range(n)[part::k]) * rows
            self.parts.append(total[at : at + size])
            at += size
        self.rows = rows

    def exchange(self, i, *others, extra=None):
        j = cube_size() - 1 - i
        if i > 0:
            self.parts = [add_pair(pair) for pair in self.pairs]
        else:
            self.cut(extra)
        halves = [x.shape[0] // 2 for x in self.parts]
        sent = after([x[h:].astype(self.kind) for x, h in zip(self.parts, halves)], *others)
        self.pairs = [
            (x[:h], fsdp_swap(y, cube_bit(part, j)))
            for part, (x, y, h) in enumerate(zip(self.parts, sent, halves))
        ]
        return [b for _, b in self.pairs]

    def line(self, *others):
        n, k = positions(), cube_size()
        slots = [None] * n
        for part, pair in enumerate(self.pairs):
            got = add_pair(pair)
            for i, r in enumerate(range(n)[part::k]):
                slots[r] = got[i * self.rows : (i + 1) * self.rows]
        sent = after([x.astype(self.kind) for x in slots[1:]], *others)
        self.arrived = line_return([slots[0]] + sent, self.kind)
        return self.arrived[1:]

    def total(self):
        return add_all(self.arrived)


def dot(a, b, dims):
    return lax.dot_general(a, b, (dims, ((), ())), preferred_element_type=F32)


NN = ((1,), (0,))
NT = ((1,), (1,))
TN = ((0,), (0,))


def turn(x, cosine, sine):
    return x * cosine + pltpu.roll(x, HEAD_SIZE // 2, 1) * sine


def causal_scores(q, k):
    scores = dot(k, q, NT) * (HEAD_SIZE ** (-0.5))
    key = lax.broadcasted_iota(jnp.int32, scores.shape, 0)
    query = lax.broadcasted_iota(jnp.int32, scores.shape, 1)
    return jnp.where(key <= query, scores, MASKED)


def cost(flops, transcendentals=0):
    return pl.CostEstimate(
        flops=int(flops), transcendentals=int(transcendentals), bytes_accessed=int(flops // 400)
    )


def attention_forward_kernel(qp, kp, vp, cosine, sine, q_out, k_out, v_out, mixed_out, lse_out):
    q = turn(qp[...], cosine[...], sine[...]).astype(BF16)
    k = turn(kp[...], cosine[...], sine[...]).astype(BF16)
    v = vp[...].astype(BF16)
    q_out[...] = q
    k_out[...] = k
    v_out[...] = v
    scores = causal_scores(q, k)
    peak = jnp.max(scores, axis=0, keepdims=True)
    expo = jnp.exp(scores - peak)
    totals = jnp.sum(expo, axis=0, keepdims=True)
    lse_out[0] = peak + jnp.log(totals)
    probability = (expo * (1.0 / totals)).astype(BF16)
    mixed_out[...] = dot(probability, v, TN).astype(BF16)


def attention_forward(projected, cosine, sine):
    length = projected.shape[0]
    width = projected.shape[1] // 3
    heads = width // HEAD_SIZE
    block = (length, HEAD_SIZE)
    table = pl.BlockSpec(block, lambda h: (0, 0))
    column = pl.BlockSpec(block, lambda h: (0, h))
    rows = jax.ShapeDtypeStruct((length, width), BF16)
    return pl.pallas_call(
        attention_forward_kernel,
        grid=(heads,),
        in_specs=[
            column,
            pl.BlockSpec(block, lambda h: (0, heads + h)),
            pl.BlockSpec(block, lambda h: (0, 2 * heads + h)),
            table,
            table,
        ],
        out_specs=[column] * 4 + [pl.BlockSpec((1, 1, length), lambda h: (h, 0, 0))],
        out_shape=[rows] * 4 + [jax.ShapeDtypeStruct((heads, 1, length), F32)],
        compiler_params=pltpu.CompilerParams(vmem_limit_bytes=VMEM_LIMIT),
        cost_estimate=cost(14e9),
        name="attention_forward",
    )(projected, projected, projected, cosine, sine)


def attention_backward_kernel(q_in, k_in, v_in, d_in, lse, cosine, sine, dq_out, dk_out, dv_out):
    q, k, v, d = q_in[...], k_in[...], v_in[...], d_in[...]
    scale = HEAD_SIZE ** (-0.5)
    probability = jnp.exp(causal_scores(q, k) - lse[0])
    dv_out[...] = dot(probability.astype(BF16), d, NN).astype(BF16)
    prob_cot = dot(v, d, NT)
    row_dot = jnp.sum(probability * prob_cot, axis=0, keepdims=True)
    score_cot = (probability * (prob_cot - row_dot)).astype(BF16)
    dk = dot(score_cot, q, NN) * scale
    dq = dot(score_cot, k, TN) * scale
    dq_out[...] = turn(dq, cosine[...], -sine[...]).astype(BF16)
    dk_out[...] = turn(dk, cosine[...], -sine[...]).astype(BF16)


def attention_backward(q, k, v, mixed_cot, lse, cosine, sine):
    length, width = q.shape
    heads = width // HEAD_SIZE
    block = (length, HEAD_SIZE)
    table = pl.BlockSpec(block, lambda h: (0, 0))
    column = pl.BlockSpec(block, lambda h: (0, h))
    return pl.pallas_call(
        attention_backward_kernel,
        grid=(heads,),
        in_specs=[column] * 4
        + [pl.BlockSpec((1, 1, length), lambda h: (h, 0, 0)), table, table],
        out_specs=[column] * 3,
        out_shape=[jax.ShapeDtypeStruct((length, width), BF16)] * 3,
        compiler_params=pltpu.CompilerParams(vmem_limit_bytes=VMEM_LIMIT),
        cost_estimate=cost(15e9),
        name="attention_backward",
    )(q, k, v, mixed_cot, lse, cosine, sine)


def silu_parts(gate_value):
    sigmoid_value = jax.nn.sigmoid(gate_value)
    return (gate_value * sigmoid_value, sigmoid_value * (1.0 + gate_value * (1.0 - sigmoid_value)))


def expert_kernel(
    first, x_own, x_other, c_own, c_other, router, weights,
    x_out, c_out, h_out, g_out, u_out, cot_own, cot_other, out_own, out_other, router_out,
    picks, xs, cs, x_cots, ys, shares, backs,
):
    length, width = x_own.shape
    capacity = x_out.shape[1] // 2
    experts = router.shape[0]
    local = pl.num_programs(0)
    count = picks.shape[1] // capacity
    step = pl.program_id(0)
    sources = ((x_own, c_own), (x_other, c_other))
    w_gate, w_up, w_down = (weights[:, 0, i].reshape(-1, width) for i in range(3))
    expert_row = lax.broadcasted_iota(jnp.int32, (experts, length), 0)
    slot_row = lax.broadcasted_iota(jnp.int32, (capacity, length), 0).astype(F32)

    def row_of(table, index):
        return jnp.sum(jnp.where(expert_row == index, table, 0.0), axis=0, keepdims=True)

    @pl.when(step == 0)
    def _():
        for at, (x_ref, c_ref) in enumerate(sources):
            ranks = c_ref[length : length + experts, :length].astype(F32)
            logits = dot(router[...], x_ref[...], NT)
            expo = jnp.exp(logits - jnp.max(logits, axis=0, keepdims=True))
            shares[at] = expo * (1.0 / jnp.sum(expo, axis=0, keepdims=True))
            pick = jnp.concatenate(
                [jnp.where(slot_row == row_of(ranks, first[0] + e), 1.0, 0.0) for e in range(count)],
                axis=0,
            ).astype(BF16)
            picks[at] = pick
            x = dot(pick, x_ref[...], NN).astype(BF16)
            c = dot(pick, c_ref[:length, :], NN).astype(BF16)
            for e in range(count):
                low, high = e * capacity, (e + 1) * capacity
                xs[e, at * capacity : (at + 1) * capacity, :] = x[low:high]
                cs[e, at * capacity : (at + 1) * capacity, :] = c[low:high]

    x = xs[step]
    c = cs[step]
    gate_columns = []
    for at, (_, c_ref) in enumerate(sources):
        ranks = c_ref[length : length + experts, :length].astype(F32)
        chosen = jnp.where(ranks >= 0.0, shares[at], 0.0)
        gate = row_of(chosen, first[0] + step) / jnp.sum(chosen, axis=0, keepdims=True)
        pick = picks[at, pl.ds(pl.multiple_of(step * capacity, 32), capacity), :].astype(F32)
        gate_columns.append(jnp.sum(pick * gate, axis=1, keepdims=True))
    gates = jnp.concatenate(gate_columns, axis=0)
    x_out[0] = x
    c_out[0] = (gates * c.astype(F32)).astype(BF16)
    gate_value = dot(x, w_gate, NT)
    up_value = dot(x, w_up, NT)
    raw_cot = dot(c, w_down, NT)
    active, slope = silu_parts(gate_value)
    hidden16 = (active * up_value).astype(BF16)
    hidden = hidden16.astype(F32)
    gate_cot = jnp.sum(raw_cot * hidden, axis=1, keepdims=True)
    hidden_cot = gates * raw_cot
    h_out[0] = hidden16
    g16 = (hidden_cot * up_value * slope).astype(BF16)
    u16 = (hidden_cot * active).astype(BF16)
    g_out[0] = g16
    u_out[0] = u16
    x_cot = (dot(g16, w_gate, NN) + dot(u16, w_up, NN)).astype(BF16)
    y = dot((gates * hidden).astype(BF16), w_down, NN).astype(BF16)
    for at in range(2):
        low, high = at * capacity, (at + 1) * capacity
        rows = pl.ds(pl.multiple_of(step * capacity, 32), capacity)
        x_cots[at, rows, :] = x_cot[low:high]
        ys[at, rows, :] = y[low:high]
        pick = picks[at, rows, :].astype(F32)
        backs[at, step] = jnp.sum(pick * gate_cot[low:high], axis=0, keepdims=True)

    @pl.when(step == local - 1)
    def _():
        for at, (x_ref, c_ref) in enumerate(sources):
            ranks = c_ref[length : length + experts, :length].astype(F32)
            probability = shares[at]
            chosen = jnp.where(ranks >= 0.0, probability, 0.0)
            total = jnp.sum(chosen, axis=0, keepdims=True)
            direct = jnp.zeros_like(chosen)
            shift = jnp.zeros_like(total)
            for e in range(count):
                back = backs[at, e]
                shift += back * row_of(chosen, first[0] + e)
                direct += jnp.where(expert_row == first[0] + e, back / total, 0.0)
            prob_cot = jnp.where(ranks >= 0.0, direct - shift / (total * total), 0.0)
            inner = jnp.sum(prob_cot * probability, axis=0, keepdims=True)
            logit_cot = (probability * (prob_cot - inner)).astype(BF16)
            cot = dot(picks[at], x_cots[at], TN) + dot(logit_cot, router[...], TN)
            out = dot(picks[at], ys[at], TN)
            (cot_own, cot_other)[at][...] = cot.astype(BF16)
            (out_own, out_other)[at][...] = out.astype(BF16)
            part = dot(logit_cot, x_ref[...], NN)
            router_out[...] = part if at == 0 else router_out[...] + part


def expert_chunk(first, x_pair, c_pair, router, weights, capacity):
    length, width = x_pair[0].shape
    pieces, local, _, part, _ = weights.shape
    units = pieces * part
    experts = router.shape[0]
    whole = lambda shape: pl.BlockSpec(
        shape, lambda e, s: (0,) * len(shape), pipeline_mode=pl.Buffered(1)
    )
    per = lambda shape: pl.BlockSpec((1,) + shape, lambda e, s: (e,) + (0,) * len(shape))
    slots = 2 * capacity
    shape = jax.ShapeDtypeStruct
    return pl.pallas_call(
        expert_kernel,
        grid_spec=pltpu.PrefetchScalarGridSpec(
            num_scalar_prefetch=1,
            grid=(local,),
            in_specs=[
                whole((length, width)),
                whole((length, width)),
                whole(c_pair[0].shape),
                whole(c_pair[1].shape),
                whole((experts, width)),
                pl.BlockSpec((pieces, 1, 3, part, width), lambda e, s: (0, e, 0, 0, 0)),
            ],
            out_specs=[per((slots, width))] * 2
            + [per((slots, units))] * 3
            + [whole((length, width))] * 4
            + [whole((experts, width))],
            scratch_shapes=[
                pltpu.VMEM((2, local * capacity, length), BF16),
                pltpu.VMEM((local, slots, width), BF16),
                pltpu.VMEM((local, slots, width), BF16),
                pltpu.VMEM((2, local * capacity, width), BF16),
                pltpu.VMEM((2, local * capacity, width), BF16),
                pltpu.VMEM((2, experts, length), F32),
                pltpu.VMEM((2, local, 1, length), F32),
            ],
        ),
        out_shape=[shape((local, slots, width), BF16)] * 2
        + [shape((local, slots, units), BF16)] * 3
        + [shape((length, width), BF16)] * 4
        + [shape((experts, width), F32)],
        compiler_params=pltpu.CompilerParams(vmem_limit_bytes=VMEM_LIMIT),
        cost_estimate=cost(5e9 * 6 * slots * local / 768),
        name="expert_chunk",
    )(first.reshape(1), *x_pair, *c_pair, router, weights)


def expert_weights_kernel(*refs):
    *inputs, out = refs
    n = len(inputs) // 5
    x, c, h, g, u = (inputs[i * n : (i + 1) * n] for i in range(5))
    for i, (left, right) in enumerate(((g, x), (u, x), (h, c))):

        @pl.when(pl.program_id(1) == i)
        def _():
            rows = [jnp.concatenate([a[0] for a in side], axis=0) for side in (left, right)]
            total = dot(*rows, TN)
            out[:, 0, 0] = total.astype(BF16).reshape(out.shape[0], out.shape[3], out.shape[4])


def expert_weight_grads(chunks, pieces):
    arrays = [a[i] for i in range(5) for a in chunks]
    local, _, width = chunks[0][0].shape
    units = chunks[0][2].shape[2]
    part = units // pieces
    slots = sum(a[0].shape[1] for a in chunks)
    return pl.pallas_call(
        expert_weights_kernel,
        grid=(local, 3),
        in_specs=[pl.BlockSpec((1,) + a.shape[1:], lambda e, i: (e, 0, 0)) for a in arrays],
        out_specs=pl.BlockSpec((pieces, 1, 1, part, width), lambda e, i: (0, e, i, 0, 0)),
        out_shape=jax.ShapeDtypeStruct((pieces, local, 3, part, width), BF16),
        compiler_params=pltpu.CompilerParams(vmem_limit_bytes=VMEM_LIMIT),
        cost_estimate=cost(2 * 6 * local * slots * units * width),
        name="expert_weights",
    )(*arrays)


def shared_kernel(x, c, c_rel, weights, order, out, back, own, other):
    width, columns = weights.shape
    units = columns // 3
    half = width // 2
    gate_value = dot(x[...], weights[:, :units], NN)
    up = dot(x[...], weights[:, units : 2 * units], NN)
    active, slope = silu_parts(gate_value)
    hidden = (active * up).astype(BF16)
    cot = dot(c[...], weights[:, 2 * units :], NN)
    gate_cot = (cot * up * slope).astype(BF16)
    up_cot = (cot * active).astype(BF16)
    out[...] = dot(hidden, weights[:, 2 * units :], NT)
    back[...] = dot(gate_cot, weights[:, :units], NT) + dot(
        up_cot, weights[:, units : 2 * units], NT
    )
    rel = dot(x[...], order[...], NN).astype(BF16)
    for cut, grad in ((slice(0, half), own), (slice(half, width), other)):
        grad[:, :units] = dot(rel[:, cut], gate_cot, TN).astype(BF16)
        grad[:, units : 2 * units] = dot(rel[:, cut], up_cot, TN).astype(BF16)
        grad[:, 2 * units :] = dot(c_rel[:, cut], hidden, TN).astype(BF16)


def shared_expert(x, c, c_rel, weights, order):
    width, columns = weights.shape
    shape = jax.ShapeDtypeStruct
    return pl.pallas_call(
        shared_kernel,
        out_shape=[shape(x.shape, F32)] * 2 + [shape((width // 2, columns), BF16)] * 2,
        compiler_params=pltpu.CompilerParams(vmem_limit_bytes=VMEM_LIMIT),
        cost_estimate=cost(30e9),
        name="shared_expert",
    )(x, c, c_rel, weights, order)


def split_matmul(values, matrix, dims):
    high = values.astype(BF16)
    low = (values - high.astype(F32)).astype(BF16)
    return dot(high, matrix, dims) + dot(low, matrix, dims)


def exact_matmul(values, matrix, dims):
    return lax.dot_general(
        values, matrix.astype(F32), (dims, ((), ())),
        precision=lax.Precision.HIGHEST, preferred_element_type=F32,
    )


def shards(
    tokens,
    out_cotangent,
    assignment,
    norm_gains,
    attention_weights,
    router_weights,
    shared_weights,
    expert_weights,
):
    length, width = tokens.shape
    rows = attention_weights.shape[0]
    ranks = lax.axis_size("dp")
    local = expert_weights.shape[0]
    experts = local * ranks
    capacity = length * 6 // experts
    units = shared_weights.shape[2]

    n, k = positions(), cube_size()
    half = width // 2
    halves = (slice(0, half), slice(half, width))

    small = jnp.concatenate([norm_gains, router_weights], axis=1)
    small = jnp.pad(small, ((0, 0), (0, LANES - small.shape[1])))
    packed_in = jnp.concatenate([attention_weights[:, :3].reshape(rows, 3 * width), small], axis=1)
    packed_out = attention_weights[:, 3]
    turned = jnp.transpose(expert_weights, (0, 1, 3, 2))
    slots_in = line_fetch(packed_in)

    hot = jnp.sum(
        (assignment[:, :, None] == jnp.arange(experts)[None, None, :]).astype(F32), axis=1
    )
    before = (jnp.arange(length)[:, None] < jnp.arange(length)[None, :]).astype(BF16)
    earlier = dot(hot.astype(BF16), before, TN)
    places = jnp.where(hot.T > 0, jnp.minimum(earlier, float(capacity)), -1.0).astype(BF16)
    places = jnp.pad(places, ((0, 0), (0, width - length)))
    sent = jnp.concatenate([out_cotangent, places], axis=0)

    owner = block_order()
    true_row = (owner[:, None] * rows + jnp.arange(rows)[None, :]).reshape(width)
    order = (jnp.arange(width)[:, None] == true_row[None, :]).astype(BF16)
    tokens_float = tokens.astype(F32)
    tokens_rel = dot(tokens, order, NN).astype(BF16)
    c_rel = dot(out_cotangent, order, NN).astype(BF16)
    root_one = lax.rsqrt(jnp.mean(tokens_float * tokens_float, axis=-1, keepdims=True) + EPSILON)
    position = jnp.arange(length).astype(F32)
    frequency = 10000.0 ** (-jnp.arange(HEAD_SIZE // 2).astype(F32) * (2.0 / HEAD_SIZE))
    angle = position[:, None] * frequency[None, :]
    cosine = jnp.concatenate([jnp.cos(angle), jnp.cos(angle)], axis=1)
    sine = jnp.concatenate([-jnp.sin(angle), jnp.sin(angle)], axis=1)
    done = [slots_in, sent, order, tokens_rel, c_rel, root_one, cosine, sine]

    gather_in = DenseGather(after(slots_in, *done))
    line_out = LineGather(packed_out)
    for j in range(k):
        if j > 0:
            gather_in.join()
        got = gather_in.exchange(*done)
        swapped = [gather_in.swap_held(*done)] if j == k - 1 else []
        going = []
        while len(line_out.right) < n and (j == k - 1 or len(line_out.right) < 2):
            going = line_out.step(*(done if len(line_out.right) < 3 else []))
        done = [got, swapped, going]
    swapped = gather_in.swap_got(*done)
    slots_out = [line_out.slot(r) for r in range(n)]
    gather_out = DenseGather(slots_out)
    gather_out.exchange(*done)
    cots = LineGather(sent)
    going = cots.step(*done)
    packed_full = jnp.concatenate(gather_in.pieces(), axis=0)
    project, small_full = packed_full[:, : 3 * width], packed_full[:, 3 * width :]

    small_true = dot(order, small_full, NN)
    gain_one = small_full[:, 0].astype(F32)
    gain_two = small_true[:, 1]
    router = small_true[:, 2 : 2 + experts].T.astype(BF16)
    unit_one = tokens_rel.astype(F32) * root_one
    normed_one = (unit_one * gain_one).astype(BF16)
    routed = lax.all_gather(after(turned, *done), "fsdp", axis=0)
    projected = dot(normed_one, project, NN)
    done = [swapped, gather_out.got, projected]
    projected = after(projected, *done)
    for j in range(1, k):
        gather_out.join()
        projected = after(projected, *gather_out.held)
        gather_out.exchange(*done)
        done = [gather_out.got]
    query, key, value, mixed, lse = attention_forward(projected, cosine, sine)
    done = [gather_out.got, mixed, going]

    swapped = gather_out.swap_all(*done)
    if len(cots.right) < n:
        cots.step(*done)
    mixed_rel = dot(after(mixed, *done), order, NN).astype(BF16)
    out_full = gather_out.columns(0, width)
    hidden_res = tokens_float + dot(mixed_rel, out_full, NN)
    root_two = lax.rsqrt(jnp.mean(hidden_res * hidden_res, axis=-1, keepdims=True) + EPSILON)
    unit_two = hidden_res * root_two
    normed_two = (unit_two * gain_two).astype(BF16)
    done = [normed_two]

    rows_two = LineGather(normed_two)
    me = lax.axis_index("dp")
    chunks, x_pairs, c_pairs = [None] * n, [None] * n, [None] * n

    def pair_up(r, *others):
        x, c = rows_two.slot(r, *others), cots.slot(r, *others)
        x_pairs[r], c_pairs[r] = (x, core_swap(x)), (c, core_swap(c))
        return x_pairs[r], c_pairs[r]

    def chunk(r, *others):
        x, c = after((x_pairs[r], c_pairs[r]), *others)
        chunks[r] = expert_chunk((me * local).astype(jnp.int32), x, c, router, routed, capacity)
        return chunks[r]

    def shared_part(*others):
        rows_ = after(normed_two, *others)
        out, back, *grad = shared_expert(rows_, out_cotangent, c_rel, shared_full, order)
        return out, back, grad

    for at in range(n - 1):
        if at == n - 2:
            done = [pair_up(n // 2, *done)]
        going = [rows_two.step(*done), cots.right[-1], cots.left[-1]]
        if at > 0 and len(cots.right) < n:
            going.append(cots.step(*done))
        beside = []
        if at == n - 4:
            beside.append(pair_up(0, *done))
        elif at == n - 3:
            beside.append(chunk(0, *done)[9])
        elif at == n - 2:
            beside.append(chunk(n // 2, *done)[9])
        done = [going, beside]

    early = sorted({1, n - 1})
    late = [r for r in range(n) if r not in early and chunks[r] is None]
    back, back_slots = LineScatter(), [None] * n
    out_sums, out_slots = LineScatter(), [None] * n

    def own_part(r, *others):
        back_slots[r] = add_pair((chunks[r][5], core_swap(after(chunks[r][6], *others))))

    def out_part(r, *others):
        got = core_swap(after(chunks[r][8], *others))
        out_slots[r] = add_pair((chunks[r][7], got))
        return got

    shared_full = lax.all_gather(
        after(shared_weights.reshape(rows, 3 * units), *done), ("dp", "fsdp"), axis=0, tiled=True
    )
    done = [pair_up(early[0], *done)]
    for at, r in enumerate(early):
        moved = [pair_up(q, *done) for q in (early + late)[at + 1 :][:1]]
        done = [chunk(r, *done)[9], moved]
    for r in range(n):
        if chunks[r] is not None:
            own_part(r)

    results = {}
    for s in range(1, n):
        going = back.step(back_slots[n - s], back_slots[s], *done)
        held = back.sent
        made = []
        wanted = [r for r in late if r in (s + 1, n - s - 1)] or ([0] if late == [0] else [])
        for r in [r for r in range(n) if chunks[r] is not None and out_slots[r] is None][:2]:
            made.append(out_part(r, *held))
        for r in wanted:
            late.remove(r)
            if x_pairs[r] is None:
                pair_up(r, *held)
            made.append(chunk(r, *held)[9])
        if not late and not wanted:
            if "shared" not in results:
                results["shared"] = shared_part(*held)
                made.append(results["shared"])
            elif "experts" not in results:
                weights = expert_weight_grads(after(chunks, *held), lax.axis_size("fsdp"))
                scatter = DenseScatter(*results["shared"][2])
                results["experts"] = weights
                made += [weights, scatter.swap(*held)]
            elif "exchange" not in results:
                results["experts"] = lax.psum_scatter(
                    after(results["experts"], *done), "fsdp", scatter_dimension=0
                )
                results["exchange"] = scatter.exchange(0, *done)
                made.append(results["exchange"])
        done = [going, made]
        for r in wanted:
            own_part(r, *done)
    for r in range(n):
        if out_slots[r] is None:
            out_part(r, *done)
    expert_sum = results["experts"]
    shared_out, shared_back, _ = results["shared"]
    back_sum = back.total(back_slots[0])
    router_part = sum(a[9] for a in chunks)

    going_out = out_sums.step(out_slots[n - 1], out_slots[1], *done) if n > 1 else []
    cotangent = out_cotangent.astype(F32)
    normed_two_cot = back_sum + shared_back
    scaled = normed_two_cot * gain_two
    gain_two_grad = jnp.sum(normed_two_cot * unit_two, axis=0)
    hidden_cot = cotangent + root_two * (
        scaled - unit_two * jnp.mean(scaled * unit_two, axis=-1, keepdims=True)
    )
    attn_cot = hidden_cot.astype(BF16)
    moved = [scatter.exchange(i, *done) for i in range(1, k)]
    mixed_cot = dot(dot(attn_cot, out_full, NT).astype(BF16), order, NT).astype(BF16)
    cot_parts = attention_backward(query, key, value, mixed_cot, lse, cosine, sine)
    done = [cot_parts, going_out, moved]

    cot_parts = after(cot_parts, *done)
    going_out = out_sums.step(out_slots[n - 2], out_slots[2], *done) if n > 2 else []
    projected_cot = jnp.concatenate(cot_parts, axis=1)
    in_grad = [dot(normed_one[:, cut], projected_cot, TN).astype(BF16) for cut in halves[::-1]]
    in_scatter = DenseScatter(in_grad[1], in_grad[0])
    swap_in = in_scatter.swap()
    out_grad = [dot(after(mixed_rel, *in_grad)[:, cut], attn_cot, TN).astype(BF16) for cut in halves]
    out_scatter = DenseScatter(*out_grad)
    swap_out = out_scatter.swap()
    true_part = exact_matmul(
        jnp.concatenate([gain_two_grad[None, :], router_part], axis=0), order, NN
    )
    done = [swap_in, swap_out]

    for i in range(k):
        going = [in_scatter.exchange(i, *done)]
        if i == 0:
            normed_one_cot = dot(after(projected_cot, *done), project, NT)
            scaled_one = normed_one_cot * gain_one
            gain_one_grad = jnp.sum(normed_one_cot * unit_one, axis=0)
            small_grad = jnp.concatenate([gain_one_grad[None, :], true_part], axis=0)
            small_grad = jnp.pad(small_grad, ((0, LANES - small_grad.shape[0]), (0, 0))).T
            small_scatter = DenseScatter(small_grad[:half], small_grad[half:], F32)
            token_part = root_one * (
                scaled_one - unit_one * jnp.mean(scaled_one * unit_one, axis=-1, keepdims=True)
            )
            token_gradient = hidden_cot + split_matmul(token_part, order, NT)
            going += [token_gradient, small_grad]
            for s in range(3, n):
                going_out = out_sums.step(out_slots[n - s], out_slots[s], *done, normed_one_cot)
            going.append(going_out)
        elif i == 1:
            going += [scatter.line(*done), expert_sum, small_scatter.swap(*done)]
        done = [going]
    last = [in_scatter.line(*done)]
    last += [
        out_scatter.exchange(i, *done, extra=small_scatter if i == 0 else None) for i in range(k)
    ]
    out_scatter.line()
    shared_gradient = scatter.total().reshape(rows, 3, units)
    in_gradient = in_scatter.total().reshape(rows, 3, width)
    out_total = out_scatter.total()
    out_gradient = out_total[:, :width]
    attention_gradient = jnp.concatenate([in_gradient, out_gradient[:, None, :]], axis=1)
    small_gradient = out_total[:, width:]
    out_sum = out_sums.total(out_slots[0])
    block_output = (hidden_res + shared_out + out_sum).astype(BF16)
    expert_gradient = jnp.transpose(expert_sum, (0, 1, 3, 2)).astype(F32)
    return (
        block_output,
        token_gradient,
        small_gradient[:, :2],
        attention_gradient,
        small_gradient[:, 2 : 2 + experts],
        shared_gradient,
        expert_gradient,
    )


def solution(mesh):
    both = ("dp", "fsdp")
    return jax.shard_map(
        shards,
        mesh=mesh,
        in_specs=(
            P(both, None),
            P(both, None),
            P(both, None),
            P(both, None),
            P(both, None, None),
            P(both, None),
            P(both, None, None),
            P("dp", None, None, "fsdp"),
        ),
        out_specs=(
            P(both, None),
            P(both, None),
            P(both, None),
            P(both, None, None),
            P(both, None),
            P(both, None, None),
            P("dp", None, None, "fsdp"),
        ),
        check_vma=False,
    )
```

```python
import jax
import jax.numpy as jnp
from jax import lax
from jax.experimental import pallas as pl
from jax.experimental.pallas import tpu as pltpu
from jax.sharding import PartitionSpec as P

HEAD_SIZE = 128
TOPK = 7
EPSILON = 1e-06
MASKED = -1e30
LANES = 128
F32 = jnp.float32
BF16 = jnp.bfloat16
VMEM_LIMIT = 58 * 1024 * 1024


def after(values, *others):
    return lax.optimization_barrier((values, others))[0]


def core_swap(x):
    return lax.ppermute(x, "dp", [(d, d ^ 1) for d in range(lax.axis_size("dp"))])


def fsdp_swap(x, bit):
    return lax.ppermute(x, "fsdp", [(f, f ^ bit) for f in range(lax.axis_size("fsdp"))])


def positions():
    return lax.axis_size("dp") // 2


def line_fetch(x):
    n = positions()
    pairs = lambda r: [
        (2 * ((p + r) % n) + c, 2 * p + c) for p in range(n) for c in range(2)
    ]
    return [x] + [lax.ppermute(x, "dp", pairs(r)) for r in range(1, n)]


def line_return(slots, kind=BF16):
    n = positions()
    pairs = lambda r: [
        (2 * p + c, 2 * ((p + r) % n) + c) for p in range(n) for c in range(2)
    ]
    return [slots[0]] + [lax.ppermute(slots[r].astype(kind), "dp", pairs(r)) for r in range(1, n)]


def add_all(parts):
    return sum(a.astype(F32) for a in parts)


def line_send(x, step, first, last):
    pairs = [(2 * p + c, 2 * (p + step) + c) for p in range(first, last + 1) for c in range(2)]
    return lax.ppermute(x, "dp", pairs)


class LineGather:
    def __init__(self, x):
        self.right, self.left = [x], [x]
        self.n = positions()

    def step(self, *others):
        s = len(self.right)
        a, b = after((self.right[-1], self.left[-1]), *others)
        self.right.append(line_send(a, 1, s - 1, self.n - 2))
        self.left.append(line_send(b, -1, 1, self.n - s))
        return self.right[-1], self.left[-1]

    def slot(self, r, *others):
        if r == 0:
            return after(self.right[0], *others)
        p = lax.axis_index("dp") // 2
        near, far = after((self.left[r], self.right[self.n - r]), *others)
        return jnp.where(p + r < self.n, near, far)


class LineScatter:
    def __init__(self):
        self.right = self.left = None
        self.s = 0
        self.n = positions()

    def step(self, to_right, to_left, *others):
        self.s += 1
        s = self.s
        a, b = after((to_right, to_left), *others)
        if self.right is not None:
            a, b = a.astype(F32) + self.right.astype(F32), b.astype(F32) + self.left.astype(F32)
        a, b = lax.optimization_barrier((a.astype(BF16), b.astype(BF16)))
        self.sent = a, b
        self.right = line_send(a, 1, 0, s - 1)
        self.left = line_send(b, -1, self.n - s, self.n - 1)
        return self.right, self.left

    def total(self, own):
        if self.right is None:
            return own.astype(F32)
        return own.astype(F32) + self.right.astype(F32) + self.left.astype(F32)


def cube_size():
    return max(lax.axis_size("fsdp").bit_length() - 1, 1)


def cube_bit(part, j):
    return 1 << ((part + j) % cube_size())


def cube_masks(part):
    masks = [0]
    for j in range(cube_size()):
        masks = masks + [m ^ cube_bit(part, j) for m in masks]
    return masks


def add_pair(pair):
    return pair[0].astype(F32) + pair[1].astype(F32)


def dense_parts(slots):
    k = cube_size()
    return [jnp.concatenate(slots[part::k], axis=0) for part in range(k)]


class DenseGather:
    def __init__(self, slots):
        self.held = dense_parts(slots)
        self.j = 0

    def exchange(self, *others):
        self.held = after(self.held, *others)
        self.got = [fsdp_swap(a, cube_bit(part, self.j)) for part, a in enumerate(self.held)]
        self.j += 1
        return self.got

    def join(self):
        self.held = [jnp.concatenate(pair, axis=0) for pair in zip(self.held, self.got)]

    def swap_held(self, *others):
        self.first = core_swap(after(jnp.concatenate(self.held, axis=0), *others))
        return self.first

    def swap_got(self, *others):
        self.second = core_swap(after(jnp.concatenate(self.got, axis=0), *others))
        return self.second

    def swap_all(self, *others):
        both = jnp.concatenate(self.held + self.got, axis=0)
        both = core_swap(after(both, *others))
        size = sum(a.shape[0] for a in self.held)
        self.first, self.second = both[:size], both[size:]
        return both

    def pieces(self):
        own, other, at = [], [], 0
        for a, b in zip(self.held, self.got):
            size = a.shape[0]
            own += [a, b]
            other += [self.first[at : at + size], self.second[at : at + size]]
            at += size
        return own + other

    def columns(self, start, stop):
        return jnp.concatenate([a[:, start:stop] for a in self.pieces()], axis=0)


def block_order():
    n = positions()
    d, f = lax.axis_index("dp"), lax.axis_index("fsdp")
    order = []
    for cx in range(2):
        for part in range(cube_size()):
            for m in cube_masks(part):
                for r in range(n)[part :: cube_size()]:
                    device = ((d // 2 + r) % n) * 2 + (d % 2 ^ cx)
                    order.append(device * lax.axis_size("fsdp") + (f ^ m))
    return jnp.stack(order)


class DenseScatter:
    def __init__(self, own, other, kind=BF16):
        self.own, self.other, self.kind = own, other, kind

    def swap(self, *others):
        other = after(self.other.astype(self.kind), *others)
        self.got = core_swap(other)
        return self.got

    def cut(self, extra):
        total = add_pair((self.own, self.got))
        if extra is not None:
            total = jnp.concatenate([total, add_pair((extra.own, extra.got))], axis=1)
        n, k = positions(), cube_size()
        rows = total.shape[0] // (n * 2**k)
        self.parts, at = [], 0
        for part in range(k):
            size = 2**k * len(range(n)[part::k]) * rows
            self.parts.append(total[at : at + size])
            at += size
        self.rows = rows

    def exchange(self, i, *others, extra=None):
        j = cube_size() - 1 - i
        if i > 0:
            self.parts = [add_pair(pair) for pair in self.pairs]
        else:
            self.cut(extra)
        halves = [x.shape[0] // 2 for x in self.parts]
        sent = after([x[h:].astype(self.kind) for x, h in zip(self.parts, halves)], *others)
        self.pairs = [
            (x[:h], fsdp_swap(y, cube_bit(part, j)))
            for part, (x, y, h) in enumerate(zip(self.parts, sent, halves))
        ]
        return [b for _, b in self.pairs]

    def line(self, *others):
        n, k = positions(), cube_size()
        slots = [None] * n
        for part, pair in enumerate(self.pairs):
            got = add_pair(pair)
            for i, r in enumerate(range(n)[part::k]):
                slots[r] = got[i * self.rows : (i + 1) * self.rows]
        sent = after([x.astype(self.kind) for x in slots[1:]], *others)
        self.arrived = line_return([slots[0]] + sent, self.kind)
        return self.arrived[1:]

    def total(self):
        return add_all(self.arrived)


def dot(a, b, dims):
    return lax.dot_general(a, b, (dims, ((), ())), preferred_element_type=F32)


NN = ((1,), (0,))
NT = ((1,), (1,))
TN = ((0,), (0,))


def turn(x, cosine, sine):
    return x * cosine + pltpu.roll(x, HEAD_SIZE // 2, 1) * sine


def causal_scores(q, k):
    scores = dot(k, q, NT) * (HEAD_SIZE ** (-0.5))
    key = lax.broadcasted_iota(jnp.int32, scores.shape, 0)
    query = lax.broadcasted_iota(jnp.int32, scores.shape, 1)
    return jnp.where(key <= query, scores, MASKED)


def cost(flops, transcendentals=0):
    return pl.CostEstimate(
        flops=int(flops), transcendentals=int(transcendentals), bytes_accessed=int(flops // 400)
    )


def attention_forward_kernel(qp, kp, vp, cosine, sine, q_out, k_out, v_out, mixed_out, lse_out):
    q = turn(qp[...], cosine[...], sine[...]).astype(BF16)
    k = turn(kp[...], cosine[...], sine[...]).astype(BF16)
    v = vp[...].astype(BF16)
    q_out[...] = q
    k_out[...] = k
    v_out[...] = v
    scores = causal_scores(q, k)
    peak = jnp.max(scores, axis=0, keepdims=True)
    expo = jnp.exp(scores - peak)
    totals = jnp.sum(expo, axis=0, keepdims=True)
    lse_out[0] = peak + jnp.log(totals)
    probability = (expo * (1.0 / totals)).astype(BF16)
    mixed_out[...] = dot(probability, v, TN).astype(BF16)


def attention_forward(projected, cosine, sine):
    length = projected.shape[0]
    width = projected.shape[1] // 3
    heads = width // HEAD_SIZE
    block = (length, HEAD_SIZE)
    table = pl.BlockSpec(block, lambda h: (0, 0))
    column = pl.BlockSpec(block, lambda h: (0, h))
    rows = jax.ShapeDtypeStruct((length, width), BF16)
    return pl.pallas_call(
        attention_forward_kernel,
        grid=(heads,),
        in_specs=[
            column,
            pl.BlockSpec(block, lambda h: (0, heads + h)),
            pl.BlockSpec(block, lambda h: (0, 2 * heads + h)),
            table,
            table,
        ],
        out_specs=[column] * 4 + [pl.BlockSpec((1, 1, length), lambda h: (h, 0, 0))],
        out_shape=[rows] * 4 + [jax.ShapeDtypeStruct((heads, 1, length), F32)],
        compiler_params=pltpu.CompilerParams(vmem_limit_bytes=VMEM_LIMIT),
        cost_estimate=cost(14e9),
        name="attention_forward",
    )(projected, projected, projected, cosine, sine)


def attention_backward_kernel(q_in, k_in, v_in, d_in, lse, cosine, sine, dq_out, dk_out, dv_out):
    q, k, v, d = q_in[...], k_in[...], v_in[...], d_in[...]
    scale = HEAD_SIZE ** (-0.5)
    probability = jnp.exp(causal_scores(q, k) - lse[0])
    dv_out[...] = dot(probability.astype(BF16), d, NN).astype(BF16)
    prob_cot = dot(v, d, NT)
    row_dot = jnp.sum(probability * prob_cot, axis=0, keepdims=True)
    score_cot = (probability * (prob_cot - row_dot)).astype(BF16)
    dk = dot(score_cot, q, NN) * scale
    dq = dot(score_cot, k, TN) * scale
    dq_out[...] = turn(dq, cosine[...], -sine[...]).astype(BF16)
    dk_out[...] = turn(dk, cosine[...], -sine[...]).astype(BF16)


def attention_backward(q, k, v, mixed_cot, lse, cosine, sine):
    length, width = q.shape
    heads = width // HEAD_SIZE
    block = (length, HEAD_SIZE)
    table = pl.BlockSpec(block, lambda h: (0, 0))
    column = pl.BlockSpec(block, lambda h: (0, h))
    return pl.pallas_call(
        attention_backward_kernel,
        grid=(heads,),
        in_specs=[column] * 4
        + [pl.BlockSpec((1, 1, length), lambda h: (h, 0, 0)), table, table],
        out_specs=[column] * 3,
        out_shape=[jax.ShapeDtypeStruct((length, width), BF16)] * 3,
        compiler_params=pltpu.CompilerParams(vmem_limit_bytes=VMEM_LIMIT),
        cost_estimate=cost(15e9),
        name="attention_backward",
    )(q, k, v, mixed_cot, lse, cosine, sine)


def silu_parts(gate_value):
    sigmoid_value = jax.nn.sigmoid(gate_value)
    return (gate_value * sigmoid_value, sigmoid_value * (1.0 + gate_value * (1.0 - sigmoid_value)))


def expert_kernel(
    first, x_own, x_other, c_own, c_other, router, weights,
    x_out, c_out, h_out, g_out, u_out, cot_own, cot_other, out_own, out_other, router_out,
    picks, xs, cs, x_cots, ys, shares, backs,
):
    length, width = x_own.shape
    capacity = x_out.shape[1] // 2
    experts = router.shape[0]
    local = pl.num_programs(0)
    count = picks.shape[1] // capacity
    step = pl.program_id(0)
    sources = ((x_own, c_own), (x_other, c_other))
    w_gate, w_up, w_down = (weights[:, 0, i].reshape(-1, width) for i in range(3))
    expert_row = lax.broadcasted_iota(jnp.int32, (experts, length), 0)
    slot_row = lax.broadcasted_iota(jnp.int32, (capacity, length), 0).astype(F32)

    def row_of(table, index):
        return jnp.sum(jnp.where(expert_row == index, table, 0.0), axis=0, keepdims=True)

    @pl.when(step == 0)
    def _():
        for at, (x_ref, c_ref) in enumerate(sources):
            ranks = c_ref[length : length + experts, :length].astype(F32)
            logits = dot(router[...], x_ref[...], NT)
            expo = jnp.exp(logits - jnp.max(logits, axis=0, keepdims=True))
            shares[at] = expo * (1.0 / jnp.sum(expo, axis=0, keepdims=True))
            pick = jnp.concatenate(
                [jnp.where(slot_row == row_of(ranks, first[0] + e), 1.0, 0.0) for e in range(count)],
                axis=0,
            ).astype(BF16)
            picks[at] = pick
            x = dot(pick, x_ref[...], NN).astype(BF16)
            c = dot(pick, c_ref[:length, :], NN).astype(BF16)
            for e in range(count):
                low, high = e * capacity, (e + 1) * capacity
                xs[e, at * capacity : (at + 1) * capacity, :] = x[low:high]
                cs[e, at * capacity : (at + 1) * capacity, :] = c[low:high]

    x = xs[step]
    c = cs[step]
    gate_columns = []
    for at, (_, c_ref) in enumerate(sources):
        ranks = c_ref[length : length + experts, :length].astype(F32)
        chosen = jnp.where(ranks >= 0.0, shares[at], 0.0)
        gate = row_of(chosen, first[0] + step) / jnp.sum(chosen, axis=0, keepdims=True)
        pick = picks[at, pl.ds(pl.multiple_of(step * capacity, 32), capacity), :].astype(F32)
        gate_columns.append(jnp.sum(pick * gate, axis=1, keepdims=True))
    gates = jnp.concatenate(gate_columns, axis=0)
    x_out[0] = x
    c_out[0] = (gates * c.astype(F32)).astype(BF16)
    gate_value = dot(x, w_gate, NT)
    up_value = dot(x, w_up, NT)
    raw_cot = dot(c, w_down, NT)
    active, slope = silu_parts(gate_value)
    hidden16 = (active * up_value).astype(BF16)
    hidden = hidden16.astype(F32)
    gate_cot = jnp.sum(raw_cot * hidden, axis=1, keepdims=True)
    hidden_cot = gates * raw_cot
    h_out[0] = hidden16
    g16 = (hidden_cot * up_value * slope).astype(BF16)
    u16 = (hidden_cot * active).astype(BF16)
    g_out[0] = g16
    u_out[0] = u16
    x_cot = (dot(g16, w_gate, NN) + dot(u16, w_up, NN)).astype(BF16)
    y = dot((gates * hidden).astype(BF16), w_down, NN).astype(BF16)
    for at in range(2):
        low, high = at * capacity, (at + 1) * capacity
        rows = pl.ds(pl.multiple_of(step * capacity, 32), capacity)
        x_cots[at, rows, :] = x_cot[low:high]
        ys[at, rows, :] = y[low:high]
        pick = picks[at, rows, :].astype(F32)
        backs[at, step] = jnp.sum(pick * gate_cot[low:high], axis=0, keepdims=True)

    @pl.when(step == local - 1)
    def _():
        for at, (x_ref, c_ref) in enumerate(sources):
            ranks = c_ref[length : length + experts, :length].astype(F32)
            probability = shares[at]
            chosen = jnp.where(ranks >= 0.0, probability, 0.0)
            total = jnp.sum(chosen, axis=0, keepdims=True)
            direct = jnp.zeros_like(chosen)
            shift = jnp.zeros_like(total)
            for e in range(count):
                back = backs[at, e]
                shift += back * row_of(chosen, first[0] + e)
                direct += jnp.where(expert_row == first[0] + e, back / total, 0.0)
            prob_cot = jnp.where(ranks >= 0.0, direct - shift / (total * total), 0.0)
            inner = jnp.sum(prob_cot * probability, axis=0, keepdims=True)
            logit_cot = (probability * (prob_cot - inner)).astype(BF16)
            cot = dot(picks[at], x_cots[at], TN) + dot(logit_cot, router[...], TN)
            out = dot(picks[at], ys[at], TN)
            (cot_own, cot_other)[at][...] = cot.astype(BF16)
            (out_own, out_other)[at][...] = out.astype(BF16)
            part = dot(logit_cot, x_ref[...], NN)
            router_out[...] = part if at == 0 else router_out[...] + part


def expert_chunk(first, x_pair, c_pair, router, weights, capacity):
    length, width = x_pair[0].shape
    pieces, local, _, part, _ = weights.shape
    units = pieces * part
    experts = router.shape[0]
    whole = lambda shape: pl.BlockSpec(
        shape, lambda e, s: (0,) * len(shape), pipeline_mode=pl.Buffered(1)
    )
    per = lambda shape: pl.BlockSpec((1,) + shape, lambda e, s: (e,) + (0,) * len(shape))
    slots = 2 * capacity
    shape = jax.ShapeDtypeStruct
    return pl.pallas_call(
        expert_kernel,
        grid_spec=pltpu.PrefetchScalarGridSpec(
            num_scalar_prefetch=1,
            grid=(local,),
            in_specs=[
                whole((length, width)),
                whole((length, width)),
                whole(c_pair[0].shape),
                whole(c_pair[1].shape),
                whole((experts, width)),
                pl.BlockSpec((pieces, 1, 3, part, width), lambda e, s: (0, e, 0, 0, 0)),
            ],
            out_specs=[per((slots, width))] * 2
            + [per((slots, units))] * 3
            + [whole((length, width))] * 4
            + [whole((experts, width))],
            scratch_shapes=[
                pltpu.VMEM((2, local * capacity, length), BF16),
                pltpu.VMEM((local, slots, width), BF16),
                pltpu.VMEM((local, slots, width), BF16),
                pltpu.VMEM((2, local * capacity, width), BF16),
                pltpu.VMEM((2, local * capacity, width), BF16),
                pltpu.VMEM((2, experts, length), F32),
                pltpu.VMEM((2, local, 1, length), F32),
            ],
        ),
        out_shape=[shape((local, slots, width), BF16)] * 2
        + [shape((local, slots, units), BF16)] * 3
        + [shape((length, width), BF16)] * 4
        + [shape((experts, width), F32)],
        compiler_params=pltpu.CompilerParams(vmem_limit_bytes=VMEM_LIMIT),
        cost_estimate=cost(5e9 * 6 * slots * local / 768),
        name="expert_chunk",
    )(first.reshape(1), *x_pair, *c_pair, router, weights)


def expert_weights_kernel(*refs):
    *inputs, out = refs
    n = len(inputs) // 5
    x, c, h, g, u = (inputs[i * n : (i + 1) * n] for i in range(5))
    for i, (left, right) in enumerate(((g, x), (u, x), (h, c))):

        @pl.when(pl.program_id(1) == i)
        def _():
            rows = [jnp.concatenate([a[0] for a in side], axis=0) for side in (left, right)]
            total = dot(*rows, TN)
            out[:, 0, 0] = total.astype(BF16).reshape(out.shape[0], out.shape[3], out.shape[4])


def expert_weight_grads(chunks, pieces):
    arrays = [a[i] for i in range(5) for a in chunks]
    local, _, width = chunks[0][0].shape
    units = chunks[0][2].shape[2]
    part = units // pieces
    slots = sum(a[0].shape[1] for a in chunks)
    return pl.pallas_call(
        expert_weights_kernel,
        grid=(local, 3),
        in_specs=[pl.BlockSpec((1,) + a.shape[1:], lambda e, i: (e, 0, 0)) for a in arrays],
        out_specs=pl.BlockSpec((pieces, 1, 1, part, width), lambda e, i: (0, e, i, 0, 0)),
        out_shape=jax.ShapeDtypeStruct((pieces, local, 3, part, width), BF16),
        compiler_params=pltpu.CompilerParams(vmem_limit_bytes=VMEM_LIMIT),
        cost_estimate=cost(2 * 6 * local * slots * units * width),
        name="expert_weights",
    )(*arrays)


def shared_kernel(x, c, c_rel, weights, order, out, back, own, other):
    width, columns = weights.shape
    units = columns // 3
    half = width // 2
    gate_value = dot(x[...], weights[:, :units], NN)
    up = dot(x[...], weights[:, units : 2 * units], NN)
    active, slope = silu_parts(gate_value)
    hidden = (active * up).astype(BF16)
    cot = dot(c[...], weights[:, 2 * units :], NN)
    gate_cot = (cot * up * slope).astype(BF16)
    up_cot = (cot * active).astype(BF16)
    out[...] = dot(hidden, weights[:, 2 * units :], NT)
    back[...] = dot(gate_cot, weights[:, :units], NT) + dot(
        up_cot, weights[:, units : 2 * units], NT
    )
    rel = dot(x[...], order[...], NN).astype(BF16)
    for cut, grad in ((slice(0, half), own), (slice(half, width), other)):
        grad[:, :units] = dot(rel[:, cut], gate_cot, TN).astype(BF16)
        grad[:, units : 2 * units] = dot(rel[:, cut], up_cot, TN).astype(BF16)
        grad[:, 2 * units :] = dot(c_rel[:, cut], hidden, TN).astype(BF16)


def shared_expert(x, c, c_rel, weights, order):
    width, columns = weights.shape
    shape = jax.ShapeDtypeStruct
    return pl.pallas_call(
        shared_kernel,
        out_shape=[shape(x.shape, F32)] * 2 + [shape((width // 2, columns), BF16)] * 2,
        compiler_params=pltpu.CompilerParams(vmem_limit_bytes=VMEM_LIMIT),
        cost_estimate=cost(30e9),
        name="shared_expert",
    )(x, c, c_rel, weights, order)


def split_matmul(values, matrix, dims):
    high = values.astype(BF16)
    low = (values - high.astype(F32)).astype(BF16)
    return dot(high, matrix, dims) + dot(low, matrix, dims)


def exact_matmul(values, matrix, dims):
    return lax.dot_general(
        values, matrix.astype(F32), (dims, ((), ())),
        precision=lax.Precision.HIGHEST, preferred_element_type=F32,
    )


def shards(
    tokens,
    out_cotangent,
    assignment,
    norm_gains,
    attention_weights,
    router_weights,
    shared_weights,
    expert_weights,
):
    length, width = tokens.shape
    rows = attention_weights.shape[0]
    ranks = lax.axis_size("dp")
    local = expert_weights.shape[0]
    experts = local * ranks
    capacity = length * 6 // experts
    units = shared_weights.shape[2]

    n, k = positions(), cube_size()
    half = width // 2
    halves = (slice(0, half), slice(half, width))

    small = jnp.concatenate([norm_gains, router_weights], axis=1)
    small = jnp.pad(small, ((0, 0), (0, LANES - small.shape[1])))
    packed_in = jnp.concatenate([attention_weights[:, :3].reshape(rows, 3 * width), small], axis=1)
    packed_out = attention_weights[:, 3]
    turned = jnp.transpose(expert_weights, (0, 1, 3, 2))
    slots_in = line_fetch(packed_in)

    hot = jnp.sum(
        (assignment[:, :, None] == jnp.arange(experts)[None, None, :]).astype(F32), axis=1
    )
    before = (jnp.arange(length)[:, None] < jnp.arange(length)[None, :]).astype(BF16)
    earlier = dot(hot.astype(BF16), before, TN)
    places = jnp.where(hot.T > 0, jnp.minimum(earlier, float(capacity)), -1.0).astype(BF16)
    places = jnp.pad(places, ((0, 0), (0, width - length)))
    sent = jnp.concatenate([out_cotangent, places], axis=0)

    owner = block_order()
    true_row = (owner[:, None] * rows + jnp.arange(rows)[None, :]).reshape(width)
    order = (jnp.arange(width)[:, None] == true_row[None, :]).astype(BF16)
    tokens_float = tokens.astype(F32)
    tokens_rel = dot(tokens, order, NN).astype(BF16)
    c_rel = dot(out_cotangent, order, NN).astype(BF16)
    root_one = lax.rsqrt(jnp.mean(tokens_float * tokens_float, axis=-1, keepdims=True) + EPSILON)
    position = jnp.arange(length).astype(F32)
    frequency = 10000.0 ** (-jnp.arange(HEAD_SIZE // 2).astype(F32) * (2.0 / HEAD_SIZE))
    angle = position[:, None] * frequency[None, :]
    cosine = jnp.concatenate([jnp.cos(angle), jnp.cos(angle)], axis=1)
    sine = jnp.concatenate([-jnp.sin(angle), jnp.sin(angle)], axis=1)
    done = [slots_in, sent, order, tokens_rel, c_rel, root_one, cosine, sine]

    gather_in = DenseGather(after(slots_in, *done))
    line_out = LineGather(packed_out)
    for j in range(k):
        if j > 0:
            gather_in.join()
        got = gather_in.exchange(*done)
        swapped = [gather_in.swap_held(*done)] if j == k - 1 else []
        going = []
        while len(line_out.right) < n and (j == k - 1 or len(line_out.right) < 2):
            going = line_out.step(*(done if len(line_out.right) < 3 else []))
        done = [got, swapped, going]
    swapped = gather_in.swap_got(*done)
    slots_out = [line_out.slot(r) for r in range(n)]
    gather_out = DenseGather(slots_out)
    gather_out.exchange(*done)
    cots = LineGather(sent)
    going = cots.step(*done)
    packed_full = jnp.concatenate(gather_in.pieces(), axis=0)
    project, small_full = packed_full[:, : 3 * width], packed_full[:, 3 * width :]

    small_true = dot(order, small_full, NN)
    gain_one = small_full[:, 0].astype(F32)
    gain_two = small_true[:, 1]
    router = small_true[:, 2 : 2 + experts].T.astype(BF16)
    unit_one = tokens_rel.astype(F32) * root_one
    normed_one = (unit_one * gain_one).astype(BF16)
    routed = lax.all_gather(after(turned, *done), "fsdp", axis=0)
    projected = dot(normed_one, project, NN)
    done = [swapped, gather_out.got, projected]
    projected = after(projected, *done)
    for j in range(1, k):
        gather_out.join()
        projected = after(projected, *gather_out.held)
        gather_out.exchange(*done)
        done = [gather_out.got]
    query, key, value, mixed, lse = attention_forward(projected, cosine, sine)
    done = [gather_out.got, mixed, going]

    swapped = gather_out.swap_all(*done)
    if len(cots.right) < n:
        cots.step(*done)
    mixed_rel = dot(after(mixed, *done), order, NN).astype(BF16)
    out_full = gather_out.columns(0, width)
    hidden_res = tokens_float + dot(mixed_rel, out_full, NN)
    root_two = lax.rsqrt(jnp.mean(hidden_res * hidden_res, axis=-1, keepdims=True) + EPSILON)
    unit_two = hidden_res * root_two
    normed_two = (unit_two * gain_two).astype(BF16)
    done = [normed_two]

    rows_two = LineGather(normed_two)
    me = lax.axis_index("dp")
    chunks, x_pairs, c_pairs = [None] * n, [None] * n, [None] * n

    def pair_up(r, *others):
        x, c = rows_two.slot(r, *others), cots.slot(r, *others)
        x_pairs[r], c_pairs[r] = (x, core_swap(x)), (c, core_swap(c))
        return x_pairs[r], c_pairs[r]

    def chunk(r, *others):
        x, c = after((x_pairs[r], c_pairs[r]), *others)
        chunks[r] = expert_chunk((me * local).astype(jnp.int32), x, c, router, routed, capacity)
        return chunks[r]

    def shared_part(*others):
        rows_ = after(normed_two, *others)
        out, back, *grad = shared_expert(rows_, out_cotangent, c_rel, shared_full, order)
        return out, back, grad

    for at in range(n - 1):
        if at == n - 2:
            done = [pair_up(n // 2, *done)]
        going = [rows_two.step(*done), cots.right[-1], cots.left[-1]]
        if at > 0 and len(cots.right) < n:
            going.append(cots.step(*done))
        beside = []
        if at == n - 4:
            beside.append(pair_up(0, *done))
        elif at == n - 3:
            beside.append(chunk(0, *done)[9])
        elif at == n - 2:
            beside.append(chunk(n // 2, *done)[9])
        done = [going, beside]

    early = sorted({1, n - 1})
    late = [r for r in range(n) if r not in early and chunks[r] is None]
    back, back_slots = LineScatter(), [None] * n
    out_sums, out_slots = LineScatter(), [None] * n

    def own_part(r, *others):
        back_slots[r] = add_pair((chunks[r][5], core_swap(after(chunks[r][6], *others))))

    def out_part(r, *others):
        got = core_swap(after(chunks[r][8], *others))
        out_slots[r] = add_pair((chunks[r][7], got))
        return got

    shared_full = lax.all_gather(
        after(shared_weights.reshape(rows, 3 * units), *done), ("dp", "fsdp"), axis=0, tiled=True
    )
    done = [pair_up(early[0], *done)]
    for at, r in enumerate(early):
        moved = [pair_up(q, *done) for q in (early + late)[at + 1 :][:1]]
        done = [chunk(r, *done)[9], moved]
    for r in range(n):
        if chunks[r] is not None:
            own_part(r)

    results = {}
    for s in range(1, n):
        going = back.step(back_slots[n - s], back_slots[s], *done)
        held = back.sent
        made = []
        wanted = [r for r in late if r in (s + 1, n - s - 1)] or ([0] if late == [0] else [])
        for r in [r for r in range(n) if chunks[r] is not None and out_slots[r] is None][:2]:
            made.append(out_part(r, *held))
        for r in wanted:
            late.remove(r)
            if x_pairs[r] is None:
                pair_up(r, *held)
            made.append(chunk(r, *held)[9])
        if not late and not wanted:
            if "shared" not in results:
                results["shared"] = shared_part(*held)
                made.append(results["shared"])
            elif "experts" not in results:
                weights = expert_weight_grads(after(chunks, *held), lax.axis_size("fsdp"))
                scatter = DenseScatter(*results["shared"][2])
                results["experts"] = weights
                made += [weights, scatter.swap(*held)]
            elif "exchange" not in results:
                results["experts"] = lax.psum_scatter(
                    after(results["experts"], *done), "fsdp", scatter_dimension=0
                )
                results["exchange"] = scatter.exchange(0, *done)
                made.append(results["exchange"])
        done = [going, made]
        for r in wanted:
            own_part(r, *done)
    for r in range(n):
        if out_slots[r] is None:
            out_part(r, *done)
    expert_sum = results["experts"]
    shared_out, shared_back, _ = results["shared"]
    back_sum = back.total(back_slots[0])
    router_part = sum(a[9] for a in chunks)

    going_out = out_sums.step(out_slots[n - 1], out_slots[1], *done) if n > 1 else []
    cotangent = out_cotangent.astype(F32)
    normed_two_cot = back_sum + shared_back
    scaled = normed_two_cot * gain_two
    gain_two_grad = jnp.sum(normed_two_cot * unit_two, axis=0)
    hidden_cot = cotangent + root_two * (
        scaled - unit_two * jnp.mean(scaled * unit_two, axis=-1, keepdims=True)
    )
    attn_cot = hidden_cot.astype(BF16)
    moved = [scatter.exchange(i, *done) for i in range(1, k)]
    mixed_cot = dot(dot(attn_cot, out_full, NT).astype(BF16), order, NT).astype(BF16)
    cot_parts = attention_backward(query, key, value, mixed_cot, lse, cosine, sine)
    done = [cot_parts, going_out, moved]

    cot_parts = after(cot_parts, *done)
    going_out = out_sums.step(out_slots[n - 2], out_slots[2], *done) if n > 2 else []
    projected_cot = jnp.concatenate(after(cot_parts, *(out_sums.sent if n > 2 else [])), axis=1)
    in_grad = [dot(normed_one[:, cut], projected_cot, TN).astype(BF16) for cut in halves[::-1]]
    in_scatter = DenseScatter(in_grad[1], in_grad[0])
    swap_in = in_scatter.swap()
    out_grad = [dot(after(mixed_rel, *in_grad)[:, cut], attn_cot, TN).astype(BF16) for cut in halves]
    out_scatter = DenseScatter(*out_grad)
    swap_out = out_scatter.swap()
    true_part = exact_matmul(
        jnp.concatenate([gain_two_grad[None, :], router_part], axis=0), order, NN
    )
    done = [swap_in, swap_out, going_out]

    for i in range(k):
        going = [in_scatter.exchange(i, *done)]
        if i == 0:
            normed_one_cot = dot(after(projected_cot, *done), project, NT)
            scaled_one = normed_one_cot * gain_one
            gain_one_grad = jnp.sum(normed_one_cot * unit_one, axis=0)
            small_grad = jnp.concatenate([gain_one_grad[None, :], true_part], axis=0)
            small_grad = jnp.pad(small_grad, ((0, LANES - small_grad.shape[0]), (0, 0))).T
            small_scatter = DenseScatter(small_grad[:half], small_grad[half:], F32)
            token_part = root_one * (
                scaled_one - unit_one * jnp.mean(scaled_one * unit_one, axis=-1, keepdims=True)
            )
            token_gradient = hidden_cot + split_matmul(token_part, order, NT)
            going += [token_gradient, small_grad]
            for s in range(3, n):
                going_out = out_sums.step(out_slots[n - s], out_slots[s], *done, normed_one_cot)
            going.append(going_out)
        elif i == 1:
            going += [scatter.line(*done), expert_sum, small_scatter.swap(*done)]
        done = [going]
    last = [in_scatter.line(*done)]
    last += [
        out_scatter.exchange(i, *done, extra=small_scatter if i == 0 else None) for i in range(k)
    ]
    out_scatter.line()
    shared_gradient = scatter.total().reshape(rows, 3, units)
    in_gradient = in_scatter.total().reshape(rows, 3, width)
    out_total = out_scatter.total()
    out_gradient = out_total[:, :width]
    attention_gradient = jnp.concatenate([in_gradient, out_gradient[:, None, :]], axis=1)
    small_gradient = out_total[:, width:]
    out_sum = out_sums.total(out_slots[0])
    block_output = (hidden_res + shared_out + out_sum).astype(BF16)
    expert_gradient = jnp.transpose(expert_sum, (0, 1, 3, 2)).astype(F32)
    return (
        block_output,
        token_gradient,
        small_gradient[:, :2],
        attention_gradient,
        small_gradient[:, 2 : 2 + experts],
        shared_gradient,
        expert_gradient,
    )


def solution(mesh):
    both = ("dp", "fsdp")
    return jax.shard_map(
        shards,
        mesh=mesh,
        in_specs=(
            P(both, None),
            P(both, None),
            P(both, None),
            P(both, None),
            P(both, None, None),
            P(both, None),
            P(both, None, None),
            P("dp", None, None, "fsdp"),
        ),
        out_specs=(
            P(both, None),
            P(both, None),
            P(both, None),
            P(both, None, None),
            P(both, None),
            P(both, None, None),
            P("dp", None, None, "fsdp"),
        ),
        check_vma=False,
    )
```
